32 devices in a mesh: grp: 4 (over z), ctx: 8 (over y, x, core).
Axes of the slice: x: 2, y: 2, z: 4, core: 2. Of those that a mesh axis runs over, the one named last changes fastest.
Arguments:
- query_rows: bfloat16 [32768, 512], P(('grp', 'ctx')), may hold values from -6 to 6
- key_rows: bfloat16 [32768, 512], P(('grp', 'ctx')), may hold values from -6 to 6
- value_rows: bfloat16 [32768, 512], P(('grp', 'ctx')), may hold values from -6 to 6
- cluster_ids: int32 [4, 32768], P(None, ('grp', 'ctx')), may hold values from 0 to 255, as said below
Outputs:
- attended: bfloat16 [32768, 512], P(('grp', 'ctx'))
The draws below stay inside these ranges and needn't reach their ends.
Inputs may be any that keep to these rules, and one draw needn't show every extreme that they name: `cluster_ids`: for each head, the tokens of one device whose clusters share one value of id // 8 number at most 96; for each head one such range receives exactly 96 tokens from every device, and every other range at most 32 from one device. For each head and range, the sum over its clusters of their token counts rounded up to multiples of 128 is at most 3072, with equality for the range that is full.
All inputs are finite; a program needn't handle non-finite values.
Results may differ from the reference program's by a relative error of at most 0.0034.
Values may be sent and summed in bfloat16 or wider, within the bound.
A program may use at most 128 MiB of HBM per device.

```python
import jax
import jax.numpy as jnp
from jax import lax

HEADS = 4
HD = 128
CL_DEV = 8
TILE = 128
TOK_DEV = 1024
TOKENS = 32768


def routing_plan(key):
    device_count = TOKENS // TOK_DEV
    capacity = 3 * TOK_DEV // device_count
    modest = TOK_DEV // device_count
    busy_rows = device_count * capacity
    tile_count = busy_rows // TILE
    pool_size = (device_count - 1) * modest
    root_key = jax.random.fold_in(key, 7101)
    label_list = []
    busiest_list = []
    for head_pos in range(HEADS):
        head_key = jax.random.fold_in(root_key, head_pos)
        busiest = jax.random.randint(jax.random.fold_in(head_key, 1), (), 0, device_count).astype(jnp.int32)
        pick_keys = jax.random.split(jax.random.fold_in(head_key, 2), device_count)
        picked = jax.vmap(lambda one_key: jax.random.permutation(one_key, pool_size)[:TOK_DEV - capacity])(pick_keys)
        others = (picked // modest).astype(jnp.int32)
        others = others + (others >= busiest).astype(jnp.int32)
        targets = jnp.concatenate([jnp.full((device_count, capacity), busiest, jnp.int32), others], axis=1)
        order_keys = jax.random.split(jax.random.fold_in(head_key, 3), device_count)
        targets = jax.vmap(lambda one_key, one_row: jax.random.permutation(one_key, one_row))(order_keys, targets)
        first_pick = jax.random.randint(jax.random.fold_in(head_key, 4), (device_count, TOK_DEV), 0, CL_DEV)
        second_pick = jax.random.randint(jax.random.fold_in(head_key, 5), (device_count, TOK_DEV), 0, CL_DEV)
        spread = jnp.minimum(first_pick, second_pick).astype(jnp.int32)
        cut_points = jnp.sort(jax.random.permutation(jax.random.fold_in(head_key, 6), tile_count - 1)[:CL_DEV - 1] + 1)
        row_index = jnp.arange(busy_rows, dtype=jnp.int32)
        busy_labels = jnp.sum((row_index[:, None] >= cut_points[None, :] * TILE).astype(jnp.int32), axis=1)
        busy_labels = jax.random.permutation(jax.random.fold_in(head_key, 7), busy_labels)
        at_busiest = (targets == busiest).astype(jnp.int32)
        busy_rank = jnp.cumsum(at_busiest, axis=1) - at_busiest
        source_index = jnp.arange(device_count, dtype=jnp.int32)[:, None]
        lookup = jnp.minimum(source_index * capacity + busy_rank, busy_rows - 1)
        local_ids = jnp.where(at_busiest == 1, busy_labels[lookup], spread)
        label_list.append((targets * CL_DEV + local_ids).reshape(-1).astype(jnp.int32))
        busiest_list.append(busiest)
    return jnp.stack(label_list, axis=0)


def draw_cluster_ids(key, part):
    return routing_plan(key)


def drawn(key, which):
    noise_key = jax.random.fold_in(key, 9300 + which)
    values = jnp.clip(jax.random.normal(noise_key, (TOKENS, HEADS, HD), jnp.float32), -6.0, 6.0)
    return values.reshape(TOKENS, HEADS * HD).astype(jnp.bfloat16)


def draw_query_rows(key, part):
    return drawn(key, 0)


def draw_key_rows(key, part):
    return drawn(key, 1)


def shard_levels(rng, dims, cuts, smallest, top_value):
    def one(position, parts):
        heights = jax.random.uniform(jax.random.fold_in(jax.random.fold_in(rng, 6), position), (parts,), jnp.float32, smallest / len(cuts), top_value / len(cuts))
        return jnp.repeat(jnp.exp(heights), dims[position] // parts).reshape((-1,) + (1,) * (len(dims) - position - 1))

    factor_of = one(*cuts[0])
    for cut in cuts[1:]:
        factor_of = factor_of * one(*cut)
    return factor_of


def centred(own_key, shape, width, bound, cuts=(), kind=jnp.bfloat16):
    array = jax.random.normal(own_key, shape, jnp.float32) * width
    if len(cuts) > 0:
        array = shard_levels(own_key, shape, cuts, -0.22, 0.18) * array
    return jnp.clip(array, min=-bound, max=bound).astype(kind)


def setup_inputs(seed: int = 0) -> dict:
    seeds = jax.random.split(jax.random.key(seed), 5)
    query_rows = draw_query_rows(jax.random.fold_in(seeds[4], 71), 0)
    key_rows = draw_key_rows(jax.random.fold_in(seeds[4], 71), 0)
    value_rows = centred(seeds[2], (TOKENS, HEADS * HD), 1.0, 6.0, ((0, 32),))
    cluster_ids = draw_cluster_ids(jax.random.fold_in(seeds[4], 71), 0)
    return {"query_rows": query_rows, "key_rows": key_rows, "value_rows": value_rows, "cluster_ids": cluster_ids}


NEG_FILL = -1.0e30


def head_output(query_head, key_head, value_head, labels):
    total_rows = query_head.shape[0]
    positions = jnp.arange(total_rows, dtype=jnp.int32)
    sort_order = jnp.argsort(labels * total_rows + positions).astype(jnp.int32)
    sorted_query = query_head[sort_order]
    sorted_key = key_head[sort_order]
    sorted_value = value_head[sort_order]
    sorted_label = labels[sort_order]
    previous = jnp.concatenate([jnp.full((1,), -1, jnp.int32), sorted_label[:-1]])
    region_start = lax.cummax(jnp.where(sorted_label != previous, positions, 0), axis=0)
    block_rows = 256
    first_rows = region_start.reshape(-1, block_rows)[:, 0]
    score_scale = HD ** -0.5

    def one_block(block_index):
        row_start = block_index * block_rows
        query_part = lax.dynamic_slice_in_dim(sorted_query, row_start, block_rows, 0)
        query_label = lax.dynamic_slice_in_dim(sorted_label, row_start, block_rows, 0)
        query_pos = row_start + jnp.arange(block_rows, dtype=jnp.int32)

        def key_block(key_index, state_now):
            run_max, run_sum, weighted = state_now
            key_start = key_index * block_rows
            key_part = lax.dynamic_slice_in_dim(sorted_key, key_start, block_rows, 0)
            value_part = lax.dynamic_slice_in_dim(sorted_value, key_start, block_rows, 0)
            key_label = lax.dynamic_slice_in_dim(sorted_label, key_start, block_rows, 0)
            key_pos = key_start + jnp.arange(block_rows, dtype=jnp.int32)
            scores = jnp.dot(query_part, key_part.T, preferred_element_type=jnp.float32) * score_scale
            allowed = (query_label[:, None] == key_label[None, :]) & (key_pos[None, :] <= query_pos[:, None])
            masked = jnp.where(allowed, scores, NEG_FILL)
            new_max = jnp.maximum(run_max, jnp.max(masked, axis=1))
            weights = jnp.where(allowed, jnp.exp(masked - new_max[:, None]), 0.0)
            factor = jnp.exp(run_max - new_max)
            run_sum = run_sum * factor + jnp.sum(weights, axis=1)
            weighted = weighted * factor[:, None] + jnp.dot(weights.astype(jnp.bfloat16), value_part, preferred_element_type=jnp.float32)
            return new_max, run_sum, weighted

        start_state = (jnp.full((block_rows,), NEG_FILL, jnp.float32), jnp.zeros((block_rows,), jnp.float32), jnp.zeros((block_rows, HD), jnp.float32))
        first_block = first_rows[block_index] // block_rows
        run_max, run_sum, weighted = lax.fori_loop(first_block, block_index + 1, key_block, start_state)
        return (weighted / run_sum[:, None]).astype(jnp.bfloat16)

    block_ids = jnp.arange(total_rows // block_rows, dtype=jnp.int32)
    sorted_out = lax.map(one_block, block_ids).reshape(total_rows, HD)
    return jnp.zeros_like(sorted_out).at[sort_order].set(sorted_out)


def reference(query_rows, key_rows, value_rows, cluster_ids):
    query_split = query_rows.reshape(TOKENS, HEADS, HD)
    key_split = key_rows.reshape(TOKENS, HEADS, HD)
    value_split = value_rows.reshape(TOKENS, HEADS, HD)
    outputs = []
    for head_pos in range(HEADS):
        outputs.append(head_output(query_split[:, head_pos], key_split[:, head_pos], value_split[:, head_pos], cluster_ids[head_pos]))
    return jnp.stack(outputs, axis=1).reshape(TOKENS, HEADS * HD)
```

```python
import functools
import math

import jax
import jax.numpy as jnp
from jax import lax
from jax.experimental import pallas as pl
from jax.experimental.pallas import tpu as pltpu
from jax.sharding import PartitionSpec as P

CL_SHIFT = 3
LANES = 128
SUB = 16
BLOCK = 256
NEG_FILL = -1e30
F32 = jnp.float32
BF16 = jnp.bfloat16
FACTOR = LANES**-0.5 * math.log2(math.e)
MESH = pl.DeviceIdType.MESH


def up(value, step):
    return (value + step - 1) // step * step


def shift_of(value):
    assert value & (value - 1) == 0
    return value.bit_length() - 1


class Plan:
    def __init__(self, groups, members, heads, tokens):
        self.groups, self.members, self.heads, self.tokens = groups, members, heads, tokens
        self.n = groups * members
        self.cap = tokens // self.n
        self.busy = 3 * tokens // self.n
        self.stride = up(self.cap, SUB)
        self.wide = up(self.busy, SUB)
        self.ranges = groups
        self.parts = 2
        self.rc = self.ranges // self.parts
        self.chunks = heads * self.parts
        self.rows = members * self.stride
        self.mrows = self.rc * self.stride
        self.crows = members * self.mrows
        self.wrows = members * self.wide
        self.base = self.n * self.stride
        self.spread = members // heads
        self.table = up((heads + 1) * members, SUB)
        self.holders = [c for c in range(1, groups - 2, 2)] + [groups - 2]
        self.qsets = groups - 2
        self.psets = groups // 2


def iota(shape, dim):
    return lax.broadcasted_iota(jnp.int32, shape, dim)


def dot(a, b):
    return jnp.dot(a, b, preferred_element_type=F32)


def dot_t(a, b):
    return lax.dot_general(a, b, (((1,), (1,)), ((), ())), preferred_element_type=F32)


def onehot(cond):
    return jnp.where(cond, 1.0, 0.0).astype(BF16)


def place_tokens(p, ids_ref, key_ref, wide_ref, place_ref):
    n, t = p.n, p.tokens
    blk = math.gcd(BLOCK, t)
    earlier = onehot(iota((blk, blk), 0) < iota((blk, blk), 1))
    owners, members = [], []
    for h in range(p.heads):
        owner = lax.shift_right_logical(ids_ref[h : h + 1, :], CL_SHIFT)
        owners.append(owner)
        members.append(jnp.where(iota((n, t), 0) == owner, 1.0, 0.0))
    member = jnp.concatenate(members, axis=0)
    carry = jnp.zeros((p.heads * n, 1), F32)
    slots = []
    for b in range(0, t, blk):
        piece = member[:, b : b + blk]
        slots.append(piece * (dot(piece.astype(BF16), earlier) + carry))
        carry += jnp.sum(piece, axis=1, keepdims=True)
    slot_all = jnp.concatenate(slots, axis=1)
    full = jnp.where(carry > p.cap, 1.0, 0.0)
    for h in range(p.heads):
        rows = slice(h * n, (h + 1) * n)
        owner = owners[h]
        slot = jnp.sum(slot_all[rows], axis=0, keepdims=True).astype(jnp.int32)
        is_busy = jnp.sum(members[h] * full[rows], axis=0, keepdims=True) > 0.5
        who = lax.shift_right_logical(owner, shift_of(p.ranges))
        which = owner & (p.ranges - 1)
        part = lax.shift_right_logical(which, shift_of(p.rc))
        row = part * p.crows + who * p.mrows + (which & (p.rc - 1)) * p.stride + slot
        key_ref[h : h + 1, :] = jnp.where(is_busy, p.base + slot, row)
        wide_ref[h : h + 1, :] = jnp.where(is_busy, slot, -1)
        place_ref[h : h + 1, :] = jnp.where(is_busy, -1, which * p.stride + slot)


def make_labels(p, ids_ref, wide_ref, place_ref, slab_ref):
    m, t = p.members, p.tokens
    row = iota((m * SUB, m), 0) - iota((m * SUB, m), 1) * SUB
    spread = jnp.zeros((m * SUB, LANES), F32)
    for h in range(p.heads):
        ids = ids_ref[h : h + 1, :]
        who = lax.shift_right_logical(ids, CL_SHIFT + shift_of(p.ranges))
        label = ((ids & (2**CL_SHIFT - 1)) + 1).astype(F32)
        mine = jnp.where(iota((m, t), 0) == who, label, 0.0).astype(BF16)
        spot = onehot(iota((LANES, t), 0) == place_ref[h : h + 1, :])
        spread += dot(onehot(row == h), dot_t(mine, spot).astype(BF16))
        spot = onehot(iota((LANES, t), 0) == wide_ref[h : h + 1, :])
        line = dot_t(jnp.broadcast_to(label, (m, t)).astype(BF16), spot)
        line = jnp.where(iota((m, LANES), 0) == h * p.spread, line, 0.0)
        spread += dot(onehot(row == p.heads), line.astype(BF16))
    slab_ref[...] = spread.astype(BF16).reshape(m, SUB, LANES)


def read_labels(p, rlab_ref):
    m = p.members
    total = m * SUB
    want = iota((p.table, total), 0)
    src, h = want & (m - 1), lax.shift_right_logical(want, shift_of(m))
    pick = onehot((iota((p.table, total), 1) == src * SUB + h) & (h <= p.heads))
    return dot(pick, rlab_ref[...].reshape(total, LANES))


def row_labels(table, width, offset):
    m = table.shape[0]
    total = m * width
    src = iota((m, width, m), 0).reshape(total, m)
    spread = dot(onehot(src == iota((total, m), 1)), table.astype(BF16))
    lane = iota((m, width, LANES), 1).reshape(total, LANES) + offset
    return jnp.sum(
        jnp.where(iota((total, LANES), 1) == lane, spread, 0.0), axis=1, keepdims=True
    )


def lane_labels(table, width, offset):
    m = table.shape[0]
    total = m * width
    lane = iota((1, total), 1)
    src = jnp.floor((lane.astype(F32) + 0.5) * (1.0 / width)).astype(jnp.int32)
    spot = onehot(iota((LANES, total), 0) == lane - src * width + offset)
    spread = dot(table.astype(BF16), spot)
    return jnp.sum(jnp.where(iota((m, total), 0) == src, spread, 0.0), axis=0, keepdims=True)


def attend(queries, parts):
    masked = [jnp.where(ok, dot_t(queries, k), NEG_FILL) for k, _, ok in parts]
    top = functools.reduce(jnp.maximum, [jnp.max(s, axis=1, keepdims=True) for s in masked])
    weights = [jnp.exp2((s - top) * FACTOR) for s in masked]
    total = sum(jnp.sum(w, axis=1, keepdims=True) for w in weights)
    acc = sum(dot(w.astype(BF16), v) for w, (_, v, _) in zip(weights, parts))
    return acc * (1.0 / total), top * FACTOR + jnp.log2(total)


def to_rows(column):
    count = column.shape[0] // LANES
    wide = jnp.broadcast_to(column, (column.shape[0], LANES)).reshape(count, LANES, LANES)
    eye = iota((count, LANES, LANES), 1) == iota((count, LANES, LANES), 2)
    return jnp.sum(jnp.where(eye, wide, 0.0), axis=1)


def to_columns(row):
    return jnp.transpose(jnp.broadcast_to(row, (LANES, LANES)))


def kernel(
    p, ids_ref, q_ref, k_ref, v_ref, out_ref,
    key_ref, wide_ref, place_ref, kcol_ref,
    sq, skv, swb, slab, rq, rkv, rwb, rlab, tab, tabf,
    zq, zwq, zkv, zwkv, pst, wst, pin, wpin, pinst, wpinst,
    loc, locst, wloc, wlocst, back, wback,
    plane_send, plane_recv, plane_own, one_send, one_recv, one_own,
    up_send, up_recv, down_send, down_recv, ret_send, ret_recv, tab_send, tab_recv,
):
    m_all, heads, chunks = p.members, p.heads, p.chunks
    g, m = lax.axis_index("grp"), lax.axis_index("ctx")
    pair_holder = (g < p.groups - 2) & (lax.rem(g, 2) == 1)
    last_holder = g == p.groups - 2
    holder = pair_holder | last_holder
    lifts = (g < p.groups - 2) & (lax.rem(g, 2) == 0)
    n_sets = jnp.where(holder, p.groups - 1 - g, 0)
    n_ret = lax.div(jnp.minimum(g, p.groups - 2), 2) + jnp.where(g == p.groups - 1, 1, 0)
    is_wide = lax.rem(m, p.spread) == 0
    sa, swa = pin.at[0], wpin.at[0]
    head_of = lax.div(m, p.spread)

    def member(step):
        return lax.rem(m + step, m_all)

    def remote(src, dst, send, recv, plane, who):
        return pltpu.make_async_remote_copy(
            src_ref=src, dst_ref=dst, send_sem=send, recv_sem=recv,
            device_id=(plane, who), device_id_type=MESH,
        )

    def wait_for(ref, sem):
        pltpu.make_async_copy(ref, ref, sem).wait()

    barrier = pltpu.get_barrier_semaphore()

    @pl.loop(1, m_all)
    def _(step):
        pl.semaphore_signal(barrier, inc=1, device_id=(g, member(step)), device_id_type=MESH)

    @pl.loop(1, p.groups)
    def _(step):
        pl.semaphore_signal(
            barrier, inc=1, device_id=(lax.rem(g + step, p.groups), m), device_id_type=MESH
        )

    def spread_out(kind, c, src_of, dst, own_src, own_dst):
        @pl.loop(1, m_all)
        def _(step):
            other = member(step)
            remote(
                src_of(other), dst, plane_send.at[kind, c], plane_recv.at[kind, c], g, other
            ).start()

        pltpu.make_async_copy(own_src, own_dst, plane_own.at[kind, c]).start()

    def send_q(c):
        spread_out(0, c, lambda o: sq.at[c, o], rq.at[c, :, m], sq.at[c, m], rq.at[c, :, m])

    def send_kv(c):
        spread_out(
            1, c, lambda o: skv.at[c, o], rkv.at[c, :, :, m], skv.at[c, m], rkv.at[c, :, :, m]
        )

    def send_answers(c):
        spread_out(2, c, lambda o: sa.at[c, :, o], back.at[c, m], sa.at[c, :, m], back.at[c, m])

    def wait_q(c):
        wait_for(rq.at[c, :, pl.ds(0, m_all - 1)], plane_recv.at[0, c])
        wait_for(rq.at[c, :, m], plane_own.at[0, c])

    def wait_kv(c):
        wait_for(rkv.at[c, :, :, pl.ds(0, m_all - 1)], plane_recv.at[1, c])
        wait_for(rkv.at[c, :, :, m], plane_own.at[1, c])

    def wait_answers(c):
        wait_for(back.at[c, pl.ds(0, m_all - 1)], plane_recv.at[2, c])
        wait_for(back.at[c, m], plane_own.at[2, c])

    def pack(c):
        h, part = lax.div(c, p.parts), lax.rem(c, p.parts)
        columns = pl.ds(pl.multiple_of(h * LANES, LANES), LANES)
        data = jnp.concatenate([q_ref[:, columns], k_ref[:, columns], v_ref[:, columns]], axis=1)
        select = onehot(
            iota((p.crows, p.tokens), 0) + part * p.crows == key_ref[pl.ds(h, 1), :]
        )
        moved = dot(select, data).astype(BF16)
        shape = (m_all, p.rc, p.stride, LANES)
        sq[c] = moved[:, :LANES].reshape(shape)
        skv[c, :, 0] = moved[:, LANES : 2 * LANES].reshape(shape)
        skv[c, :, 1] = moved[:, 2 * LANES :].reshape(shape)

    def pack_wide():
        for h in range(heads):
            columns = slice(h * LANES, (h + 1) * LANES)
            data = jnp.concatenate(
                [q_ref[:, columns], k_ref[:, columns], v_ref[:, columns]], axis=1
            )
            select = onehot(iota((p.wide, p.tokens), 0) == wide_ref[h : h + 1, :])
            moved = dot(select, data).astype(BF16)
            for i in range(3):
                swb[h, i] = moved[:, i * LANES : (i + 1) * LANES]
            target = h * p.spread

            @pl.when(m == target)
            def _():
                pltpu.make_async_copy(swb.at[h], rwb.at[:, m], one_own.at[0]).start()

            @pl.when(m != target)
            def _():
                remote(
                    swb.at[h], rwb.at[:, m], one_send.at[0], one_recv.at[0], g, target
                ).start()

    def wait_wide():
        wait_for(rwb.at[:, pl.ds(0, m_all - 1)], one_recv.at[0])
        wait_for(rwb.at[:, m], one_own.at[0])

    def send_labels():
        make_labels(p, ids_ref, wide_ref, place_ref, slab)

        @pl.loop(1, m_all)
        def _(step):
            other = member(step)
            remote(slab.at[other], rlab.at[m], one_send.at[1], one_recv.at[1], g, other).start()

        pltpu.make_async_copy(slab.at[m], rlab.at[m], one_own.at[1]).start()

    def share_labels():
        wait_for(rlab.at[pl.ds(0, m_all - 1)], one_recv.at[1])
        wait_for(rlab.at[m], one_own.at[1])
        mine = read_labels(p, rlab)
        tabf[g] = mine
        tab[g] = mine.astype(BF16)
        for c, holding in enumerate(p.holders):

            @pl.when(g > holding)
            def _():
                remote(tab.at[g], tab.at[g], tab_send.at[c], tab_recv.at[g], holding, m).start()

        @pl.when(lifts)
        def _():
            remote(
                tab.at[g], tab.at[g], tab_send.at[len(p.holders)], tab_recv.at[g], g + 1, m
            ).start()

    def fetch_labels():
        def fetch(s):
            wait_for(tab.at[s], tab_recv.at[s])
            tabf[s] = tab[s].astype(F32)

        @pl.when(pair_holder)
        def _():
            fetch(g - 1)

        @pl.loop(0, n_sets)
        def _(i):
            fetch(g + 1 + i)

    def forward(c):
        wait_q(c)
        for i, holding in enumerate(p.holders):

            @pl.when(g > holding)
            def _():
                s = g - holding - 1
                remote(
                    rq.at[c], zq.at[s, c], down_send.at[i, c], down_recv.at[s, c], holding, m
                ).start()

    def lift(c):
        @pl.when(lifts)
        def _():
            remote(rkv.at[c], zkv.at[c], up_send.at[c], up_recv.at[c], g + 1, m).start()

    def forward_wide():
        @pl.when(is_wide)
        def _():
            wait_wide()
            for i, holding in enumerate(p.holders):

                @pl.when(g > holding)
                def _():
                    s = g - holding - 1
                    remote(
                        rwb.at[0], zwq.at[s], down_send.at[i, chunks],
                        down_recv.at[s, chunks], holding, m,
                    ).start()

            @pl.when(lifts)
            def _():
                remote(
                    rwb.at[pl.ds(1, 2)], zwkv, up_send.at[chunks], up_recv.at[chunks], g + 1, m
                ).start()

    def tables(s, h):
        return tabf[s, pl.ds(pl.multiple_of(h * m_all, m_all), m_all), :]

    def flat(value):
        return value.reshape(-1, LANES)

    def causal(size, keys, first):
        return iota((size, keys), 1) <= iota((size, keys), 0) + first

    def return_part(pin_ref, pinst_ref, src, st, s, slot):
        target = g + 1 + s
        where = jnp.where(last_holder, p.psets - 1, lax.div(g - 1, 2))
        remote(
            src, pin_ref(where), ret_send.at[0, s, slot], ret_recv.at[0, where, slot], target, m
        ).start()
        remote(
            st, pinst_ref(where), ret_send.at[1, s, slot], ret_recv.at[1, where, slot], target, m
        ).start()

    def tile_of(c):
        return lax.div(c, p.parts), lax.rem(c, p.parts) * p.rc

    def own_part(c, with_before):
        h, r = tile_of(c)
        for j in range(p.rc):
            offset = (r + j) * p.stride
            table = tables(g, h)
            lq, lk = row_labels(table, p.stride, offset), lane_labels(table, p.stride, offset)
            ok = (lq == lk) & causal(p.rows, p.rows, 0)
            parts = [(flat(rkv[c, 0, j]), flat(rkv[c, 1, j]), ok)]
            if with_before:
                before = lane_labels(tables(g - 1, h), p.stride, offset)
                parts.append((flat(zkv[c, 0, j]), flat(zkv[c, 1, j]), lq == before))
            out, lse = attend(flat(rq[c, j]), parts)

            @pl.when(n_ret == 0)
            def _():
                sa[c, j] = out.astype(BF16).reshape(m_all, p.stride, LANES)

            @pl.when(n_ret > 0)
            def _():
                loc[c, j] = out
                count = p.rows // LANES
                locst[c, j * count : (j + 1) * count, :] = to_rows(lse)

        @pl.when(n_ret == 0)
        def _():
            send_answers(c)

    def visitors(c, with_before):
        h, r = tile_of(c)

        @pl.loop(0, n_sets)
        def _(s):
            wait_for(zq.at[s, c], down_recv.at[s, c])
            for j in range(p.rc):
                offset = (r + j) * p.stride
                lq = row_labels(tables(g + 1 + s, h), p.stride, offset)
                lk = lane_labels(tables(g, h), p.stride, offset)
                parts = [(flat(rkv[c, 0, j]), flat(rkv[c, 1, j]), lq == lk)]
                if with_before:
                    before = lane_labels(tables(g - 1, h), p.stride, offset)
                    parts.append((flat(zkv[c, 0, j]), flat(zkv[c, 1, j]), lq == before))
                out, lse = attend(flat(zq[s, c, j]), parts)
                zq[s, c, j] = out.astype(BF16).reshape(m_all, p.stride, LANES)
                count = p.rows // LANES
                pst[s, c, j * count : (j + 1) * count, :] = to_rows(lse)
            return_part(
                lambda w: pin.at[w, c], lambda w: pinst.at[w, c], zq.at[s, c], pst.at[s, c], s, c
            )

    def wide_blocks():
        size = math.gcd(BLOCK, p.wrows)
        return size, range(0, p.wrows, size)

    def own_wide(with_before):
        size, starts = wide_blocks()
        table = tables(g, heads)
        lq_all, lk_all = row_labels(table, p.wide, 0), lane_labels(table, p.wide, 0)
        queries = flat(rwb[0])
        keys, values = flat(rwb[1]), flat(rwb[2])
        outs, lses = [], []
        for first in starts:
            lq = lq_all[first : first + size]
            end = first + size
            ok = (lq == lk_all[:, :end]) & causal(size, end, first)
            parts = [(keys[:end], values[:end], ok)]
            if with_before:
                before = lane_labels(tables(g - 1, heads), p.wide, 0)
                parts.append((flat(zwkv[0]), flat(zwkv[1]), lq == before))
            out, lse = attend(queries[first:end], parts)
            outs.append(out)
            lses.append(to_rows(lse))
        out = jnp.concatenate(outs, axis=0)

        @pl.when(n_ret == 0)
        def _():
            swa[...] = out.astype(BF16).reshape(m_all, p.wide, LANES)
            send_wide()

        @pl.when(n_ret > 0)
        def _():
            wloc[...] = out
            wlocst[0 : p.wrows // LANES, :] = jnp.concatenate(lses, axis=0)

    def visitors_wide(with_before):
        size, starts = wide_blocks()

        @pl.loop(0, n_sets)
        def _(s):
            wait_for(zwq.at[s], down_recv.at[s, chunks])
            lq_all = row_labels(tables(g + 1 + s, heads), p.wide, 0)
            lk = lane_labels(tables(g, heads), p.wide, 0)
            queries = flat(zwq[s])
            outs, lses = [], []
            for first in starts:
                lq = lq_all[first : first + size]
                parts = [(flat(rwb[1]), flat(rwb[2]), lq == lk)]
                if with_before:
                    before = lane_labels(tables(g - 1, heads), p.wide, 0)
                    parts.append((flat(zwkv[0]), flat(zwkv[1]), lq == before))
                out, lse = attend(queries[first : first + size], parts)
                outs.append(out.astype(BF16))
                lses.append(to_rows(lse))
            zwq[s] = jnp.concatenate(outs, axis=0).reshape(m_all, p.wide, LANES)
            wst[s, 0 : p.wrows // LANES, :] = jnp.concatenate(lses, axis=0)
            return_part(
                lambda w: wpin.at[w], lambda w: wpinst.at[w], zwq.at[s], wst.at[s], s, chunks
            )

    def send_wide():
        @pl.loop(1, m_all)
        def _(step):
            other = member(step)
            remote(
                swa.at[other], wback.at[head_of], one_send.at[2], one_recv.at[2], g, other
            ).start()

        pltpu.make_async_copy(swa.at[m], wback.at[head_of], one_own.at[2]).start()

    def merge(outs, lses):
        top = functools.reduce(jnp.maximum, lses)
        weights = [jnp.exp2(x - top) for x in lses]
        share = 1.0 / sum(weights)
        weights = [w * share for w in weights]
        blocks = []
        for i in range(weights[0].shape[0]):
            rows = slice(i * LANES, (i + 1) * LANES)
            blocks.append(sum(to_columns(w[i : i + 1]) * o[rows] for w, o in zip(weights, outs)))
        return jnp.concatenate(blocks, axis=0).astype(BF16)

    def combine(c):
        for k in range(1, p.psets + 1):

            @pl.when(n_ret == k)
            def _():
                for i in range(k):
                    wait_for(pin.at[i, c], ret_recv.at[0, i, c])
                    wait_for(pinst.at[i, c], ret_recv.at[1, i, c])
                count = p.rows // LANES
                for j in range(p.rc):
                    rows = slice(j * count, (j + 1) * count)
                    outs = [loc[c, j]] + [flat(pin[i, c, j]) for i in range(k)]
                    lses = [locst[c, rows, :]] + [pinst[i, c, rows, :] for i in range(k)]
                    sa[c, j] = merge(outs, lses).reshape(m_all, p.stride, LANES)

        send_answers(c)

    def combine_wide():
        for k in range(1, p.psets + 1):

            @pl.when(n_ret == k)
            def _():
                for i in range(k):
                    wait_for(wpin.at[i], ret_recv.at[0, i, chunks])
                    wait_for(wpinst.at[i], ret_recv.at[1, i, chunks])
                count = p.wrows // LANES
                outs = [wloc[...]] + [flat(wpin[i]) for i in range(k)]
                lses = [wlocst[:count, :]] + [wpinst[i, :count, :] for i in range(k)]
                swa[...] = merge(outs, lses).reshape(m_all, p.wide, LANES)

        send_wide()

    def make_columns():
        for h in range(heads):
            line = jnp.broadcast_to(key_ref[h : h + 1, :].astype(F32), (LANES, p.tokens))
            kcol_ref[h] = jnp.transpose(line).astype(jnp.int32)

    def pick(h, first, count):
        pieces = []
        for at in range(0, count, LANES):
            width = min(LANES, count - at)
            lane = iota((p.tokens, width), 1) + (first + at)
            pieces.append(onehot(lane == kcol_ref[h, :, :width]))
        return jnp.concatenate(pieces, axis=1)

    def unpack(c):
        wait_answers(c)
        h, part = lax.div(c, p.parts), lax.rem(c, p.parts)
        columns = pl.ds(pl.multiple_of(h * LANES, LANES), LANES)
        rows = dot(pick(h, part * p.crows, p.crows), flat(back[c])).astype(BF16)

        @pl.when(part == 0)
        def _():
            out_ref[:, columns] = rows

        @pl.when(part > 0)
        def _():
            out_ref[:, columns] = out_ref[:, columns] + rows

    def unpack_wide():
        @pl.when(is_wide)
        def _():
            wait_for(wback.at[pl.ds(0, heads - 1)], one_recv.at[2])
            wait_for(wback.at[head_of], one_own.at[2])

        @pl.when(jnp.logical_not(is_wide))
        def _():
            wait_for(wback, one_recv.at[2])

        for h in range(heads):
            columns = slice(h * LANES, (h + 1) * LANES)
            rows = dot(pick(h, p.base, p.wide), wback[h]).astype(BF16)
            out_ref[:, columns] = out_ref[:, columns] + rows

    place_tokens(p, ids_ref, key_ref, wide_ref, place_ref)
    pl.semaphore_wait(barrier, m_all - 1 + p.groups - 1)

    @pl.loop(0, chunks)
    def _(c):
        pack(c)
        send_q(c)
        send_kv(c)

        @pl.when(c == 0)
        def _():
            send_labels()

        @pl.when(c == 1)
        def _():
            pack_wide()

        @pl.when(c == 2)
        def _():
            share_labels()

    make_columns()
    wide_at = 3
    lag = 2

    @pl.loop(0, chunks)
    def _(c):
        forward(c)
        wait_kv(c)
        lift(c)

        @pl.when(c == wide_at - 1)
        def _():
            forward_wide()

        @pl.when(pair_holder)
        def _():
            @pl.when(c == 0)
            def _():
                fetch_labels()

            wait_for(zkv.at[c], up_recv.at[c])
            own_part(c, True)
            visitors(c, True)

            @pl.when((c == wide_at) & is_wide)
            def _():
                wait_for(zwkv, up_recv.at[chunks])
                own_wide(True)
                visitors_wide(True)

        @pl.when(jnp.logical_not(pair_holder))
        def _():
            own_part(c, False)

            @pl.when((c == wide_at) & is_wide)
            def _():
                own_wide(False)

        @pl.when(last_holder)
        def _():
            @pl.when(c == lag)
            def _():
                fetch_labels()

            @pl.when(c >= lag)
            def _():
                visitors(c - lag, False)

        @pl.when((n_ret == 0) & (c >= lag))
        def _():
            unpack(c - lag)

    @pl.when(last_holder)
    def _():
        @pl.when(is_wide)
        def _():
            visitors_wide(False)

        @pl.loop(chunks - lag, chunks)
        def _(c):
            visitors(c, False)

    @pl.when(n_ret == 0)
    def _():
        @pl.loop(chunks - lag, chunks - 1)
        def _(c):
            unpack(c)

    @pl.when(n_ret > 0)
    def _():
        @pl.loop(0, chunks)
        def _(c):
            combine(c)

            @pl.when((c == wide_at) & is_wide)
            def _():
                combine_wide()

            @pl.when(c > 0)
            def _():
                unpack(c - 1)

    unpack_wide()
    unpack(chunks - 1)

    @pl.loop(0, chunks)
    def _(c):
        wait_for(sq.at[c, pl.ds(0, m_all - 1)], plane_send.at[0, c])
        wait_for(skv.at[c, pl.ds(0, m_all - 1)], plane_send.at[1, c])
        wait_for(sa.at[c, :, pl.ds(0, m_all - 1)], plane_send.at[2, c])
        for i, holding in enumerate(p.holders):

            @pl.when(g > holding)
            def _():
                wait_for(rq.at[c], down_send.at[i, c])

        @pl.when(lifts)
        def _():
            wait_for(rkv.at[c], up_send.at[c])

        @pl.loop(0, n_sets)
        def _(s):
            wait_for(zq.at[s, c], ret_send.at[0, s, c])
            wait_for(pst.at[s, c], ret_send.at[1, s, c])

    for i, holding in enumerate(p.holders):

        @pl.when(g > holding)
        def _():
            wait_for(tab.at[g], tab_send.at[i])

    @pl.when(lifts)
    def _():
        wait_for(tab.at[g], tab_send.at[len(p.holders)])

    wait_for(slab.at[pl.ds(0, m_all - 1)], one_send.at[1])

    @pl.when(jnp.logical_not(is_wide))
    def _():
        wait_for(swb, one_send.at[0])

    @pl.when(is_wide)
    def _():
        wait_for(swb.at[pl.ds(0, heads - 1)], one_send.at[0])
        wait_for(swa.at[pl.ds(0, m_all - 1)], one_send.at[2])
        for i, holding in enumerate(p.holders):

            @pl.when(g > holding)
            def _():
                wait_for(rwb.at[0], down_send.at[i, chunks])

        @pl.when(lifts)
        def _():
            wait_for(zwkv, up_send.at[chunks])

        @pl.loop(0, n_sets)
        def _(s):
            wait_for(zwq.at[s], ret_send.at[0, s, chunks])
            wait_for(wst.at[s], ret_send.at[1, s, chunks])


VMEM_SPEC = pl.BlockSpec(memory_space=pltpu.VMEM)


def local(query_rows, key_rows, value_rows, cluster_ids):
    groups, members = lax.axis_size("grp"), lax.axis_size("ctx")
    heads, tokens = cluster_ids.shape
    p = Plan(groups, members, heads, tokens)
    c, rc, m, st, w = p.chunks, p.rc, p.members, p.stride, p.wide
    qs, ps, hold = p.qsets, p.psets, len(p.holders)
    assert rc * p.rows // LANES <= 8 and p.wrows // LANES <= 8 and p.ranges * st <= LANES

    def half(*shape):
        return pltpu.VMEM((*shape, LANES), BF16)

    def full(*shape):
        return pltpu.VMEM((*shape, LANES), F32)

    ids = pltpu.VMEM((up(heads, 8), tokens), jnp.int32)
    dma = pltpu.SemaphoreType.DMA
    return pl.pallas_call(
        functools.partial(kernel, p),
        out_shape=jax.ShapeDtypeStruct((tokens, heads * LANES), BF16),
        in_specs=[VMEM_SPEC] * 4,
        out_specs=VMEM_SPEC,
        scratch_shapes=[
            ids, ids, ids, pltpu.VMEM((heads, tokens, LANES), jnp.int32),
            half(c, m, rc, st), half(c, m, 2, rc, st), half(heads, 3, w), half(m, SUB),
            half(c, rc, m, st), half(c, 2, rc, m, st), half(3, m, w), half(m, SUB),
            half(groups, p.table), full(groups, p.table),
            half(qs, c, rc, m, st), half(qs, m, w), half(c, 2, rc, m, st), half(2, m, w),
            full(qs, c, 8), full(qs, 8),
            half(ps, c, rc, m, st), half(ps, m, w), full(ps, c, 8), full(ps, 8),
            full(c, rc, p.rows), full(c, 8), full(p.wrows), full(8),
            half(c, m, rc, st), half(heads, w),
            dma((3, c)), dma((3, c)), dma((3, c)), dma((3,)), dma((3,)), dma((3,)),
            dma((c + 1,)), dma((c + 1,)), dma((hold, c + 1)), dma((qs, c + 1)),
            dma((2, qs, c + 1)), dma((2, ps, c + 1)), dma((hold + 1,)), dma((groups,)),
        ],
        compiler_params=pltpu.CompilerParams(
            collective_id=0, has_side_effects=True, vmem_limit_bytes=60 * 2**20
        ),
    )(cluster_ids, query_rows, key_rows, value_rows)


def solution(mesh):
    return jax.shard_map(
        local,
        mesh=mesh,
        in_specs=(
            P(("grp", "ctx"), None),
            P(("grp", "ctx"), None),
            P(("grp", "ctx"), None),
            P(None, ("grp", "ctx")),
        ),
        out_specs=P(("grp", "ctx"), None),
        check_vma=False,
    )
```

```python
import functools
import math

import jax
import jax.numpy as jnp
from jax import lax
from jax.experimental import pallas as pl
from jax.experimental.pallas import tpu as pltpu
from jax.sharding import PartitionSpec as P

CL_SHIFT = 3
LANES = 128
SUB = 16
BLOCK = 256
NEG_FILL = -1e30
F32 = jnp.float32
BF16 = jnp.bfloat16
FACTOR = LANES**-0.5 * math.log2(math.e)
MESH = pl.DeviceIdType.MESH


def up(value, step):
    return (value + step - 1) // step * step


def shift_of(value):
    assert value & (value - 1) == 0
    return value.bit_length() - 1


class Plan:
    def __init__(self, groups, members, heads, tokens):
        self.groups, self.members, self.heads, self.tokens = groups, members, heads, tokens
        self.n = groups * members
        self.cap = tokens // self.n
        self.busy = 3 * tokens // self.n
        self.stride = up(self.cap, SUB)
        self.wide = up(self.busy, SUB)
        self.ranges = groups
        self.parts = 2
        self.rc = self.ranges // self.parts
        self.chunks = heads * self.parts
        self.rows = members * self.stride
        self.mrows = self.rc * self.stride
        self.crows = members * self.mrows
        self.wrows = members * self.wide
        self.base = self.n * self.stride
        self.spread = members // heads
        self.table = up((heads + 1) * members, SUB)
        self.holders = [c for c in range(1, groups - 2, 2)] + [groups - 2]
        self.qsets = groups - 2
        self.psets = groups // 2


def iota(shape, dim):
    return lax.broadcasted_iota(jnp.int32, shape, dim)


def dot(a, b):
    return jnp.dot(a, b, preferred_element_type=F32)


def dot_t(a, b):
    return lax.dot_general(a, b, (((1,), (1,)), ((), ())), preferred_element_type=F32)


def onehot(cond):
    return jnp.where(cond, 1.0, 0.0).astype(BF16)


def place_tokens(p, ids_ref, key_ref, wide_ref, place_ref):
    n, t = p.n, p.tokens
    blk = math.gcd(BLOCK, t)
    earlier = onehot(iota((blk, blk), 0) < iota((blk, blk), 1))
    owners, members = [], []
    for h in range(p.heads):
        owner = lax.shift_right_logical(ids_ref[h : h + 1, :], CL_SHIFT)
        owners.append(owner)
        members.append(jnp.where(iota((n, t), 0) == owner, 1.0, 0.0))
    member = jnp.concatenate(members, axis=0)
    carry = jnp.zeros((p.heads * n, 1), F32)
    slots = []
    for b in range(0, t, blk):
        piece = member[:, b : b + blk]
        slots.append(piece * (dot(piece.astype(BF16), earlier) + carry))
        carry += jnp.sum(piece, axis=1, keepdims=True)
    slot_all = jnp.concatenate(slots, axis=1)
    full = jnp.where(carry > p.cap, 1.0, 0.0)
    for h in range(p.heads):
        rows = slice(h * n, (h + 1) * n)
        owner = owners[h]
        slot = jnp.sum(slot_all[rows], axis=0, keepdims=True).astype(jnp.int32)
        is_busy = jnp.sum(members[h] * full[rows], axis=0, keepdims=True) > 0.5
        who = lax.shift_right_logical(owner, shift_of(p.ranges))
        which = owner & (p.ranges - 1)
        part = lax.shift_right_logical(which, shift_of(p.rc))
        row = part * p.crows + who * p.mrows + (which & (p.rc - 1)) * p.stride + slot
        key_ref[h : h + 1, :] = jnp.where(is_busy, p.base + slot, row)
        wide_ref[h : h + 1, :] = jnp.where(is_busy, slot, -1)
        place_ref[h : h + 1, :] = jnp.where(is_busy, -1, which * p.stride + slot)


def make_labels(p, ids_ref, wide_ref, place_ref, slab_ref):
    m, t = p.members, p.tokens
    row = iota((m * SUB, m), 0) - iota((m * SUB, m), 1) * SUB
    spread = jnp.zeros((m * SUB, LANES), F32)
    for h in range(p.heads):
        ids = ids_ref[h : h + 1, :]
        who = lax.shift_right_logical(ids, CL_SHIFT + shift_of(p.ranges))
        label = ((ids & (2**CL_SHIFT - 1)) + 1).astype(F32)
        mine = jnp.where(iota((m, t), 0) == who, label, 0.0).astype(BF16)
        spot = onehot(iota((LANES, t), 0) == place_ref[h : h + 1, :])
        spread += dot(onehot(row == h), dot_t(mine, spot).astype(BF16))
        spot = onehot(iota((LANES, t), 0) == wide_ref[h : h + 1, :])
        line = dot_t(jnp.broadcast_to(label, (m, t)).astype(BF16), spot)
        line = jnp.where(iota((m, LANES), 0) == h * p.spread, line, 0.0)
        spread += dot(onehot(row == p.heads), line.astype(BF16))
    slab_ref[...] = spread.astype(BF16).reshape(m, SUB, LANES)


def read_labels(p, rlab_ref):
    m = p.members
    total = m * SUB
    want = iota((p.table, total), 0)
    src, h = want & (m - 1), lax.shift_right_logical(want, shift_of(m))
    pick = onehot((iota((p.table, total), 1) == src * SUB + h) & (h <= p.heads))
    return dot(pick, rlab_ref[...].reshape(total, LANES))


def row_labels(table, width, offset):
    m = table.shape[0]
    total = m * width
    src = iota((m, width, m), 0).reshape(total, m)
    spread = dot(onehot(src == iota((total, m), 1)), table.astype(BF16))
    lane = iota((m, width, LANES), 1).reshape(total, LANES) + offset
    return jnp.sum(
        jnp.where(iota((total, LANES), 1) == lane, spread, 0.0), axis=1, keepdims=True
    )


def lane_labels(table, width, offset):
    m = table.shape[0]
    total = m * width
    lane = iota((1, total), 1)
    src = jnp.floor((lane.astype(F32) + 0.5) * (1.0 / width)).astype(jnp.int32)
    spot = onehot(iota((LANES, total), 0) == lane - src * width + offset)
    spread = dot(table.astype(BF16), spot)
    return jnp.sum(jnp.where(iota((m, total), 0) == src, spread, 0.0), axis=0, keepdims=True)


def attend(queries, parts):
    masked = [jnp.where(ok, dot_t(queries, k), NEG_FILL) for k, _, ok in parts]
    top = functools.reduce(jnp.maximum, [jnp.max(s, axis=1, keepdims=True) for s in masked])
    weights = [jnp.exp2((s - top) * FACTOR) for s in masked]
    total = sum(jnp.sum(w, axis=1, keepdims=True) for w in weights)
    acc = sum(dot(w.astype(BF16), v) for w, (_, v, _) in zip(weights, parts))
    return acc * (1.0 / total), top * FACTOR + jnp.log2(total)


def to_rows(column):
    count = column.shape[0] // LANES
    wide = jnp.broadcast_to(column, (column.shape[0], LANES)).reshape(count, LANES, LANES)
    eye = iota((count, LANES, LANES), 1) == iota((count, LANES, LANES), 2)
    return jnp.sum(jnp.where(eye, wide, 0.0), axis=1)


def to_columns(row):
    return jnp.transpose(jnp.broadcast_to(row, (LANES, LANES)))


def kernel(
    p, ids_ref, q_ref, k_ref, v_ref, out_ref,
    key_ref, wide_ref, place_ref, kcol_ref,
    sq, skv, swb, slab, rq, rkv, rwb, rlab, tab, tabf,
    zq, zwq, zkv, zwkv, pst, wst, pin, wpin, pinst, wpinst,
    loc, locst, wloc, wlocst, back, wback,
    plane_send, plane_recv, plane_own, one_send, one_recv, one_own,
    up_send, up_recv, down_send, down_recv, ret_send, ret_recv, tab_send, tab_recv,
):
    m_all, heads, chunks = p.members, p.heads, p.chunks
    g, m = lax.axis_index("grp"), lax.axis_index("ctx")
    pair_holder = (g < p.groups - 2) & (lax.rem(g, 2) == 1)
    last_holder = g == p.groups - 2
    holder = pair_holder | last_holder
    lifts = (g < p.groups - 2) & (lax.rem(g, 2) == 0)
    n_sets = jnp.where(holder, p.groups - 1 - g, 0)
    n_ret = lax.div(jnp.minimum(g, p.groups - 2), 2) + jnp.where(g == p.groups - 1, 1, 0)
    is_wide = lax.rem(m, p.spread) == 0
    sa, swa = pin.at[0], wpin.at[0]
    head_of = lax.div(m, p.spread)

    def member(step):
        return lax.rem(m + step, m_all)

    def remote(src, dst, send, recv, plane, who):
        return pltpu.make_async_remote_copy(
            src_ref=src, dst_ref=dst, send_sem=send, recv_sem=recv,
            device_id=(plane, who), device_id_type=MESH,
        )

    def wait_for(ref, sem):
        pltpu.make_async_copy(ref, ref, sem).wait()

    barrier = pltpu.get_barrier_semaphore()

    @pl.loop(1, m_all)
    def _(step):
        pl.semaphore_signal(barrier, inc=1, device_id=(g, member(step)), device_id_type=MESH)

    @pl.loop(1, p.groups)
    def _(step):
        pl.semaphore_signal(
            barrier, inc=1, device_id=(lax.rem(g + step, p.groups), m), device_id_type=MESH
        )

    def spread_out(kind, c, src_of, dst, own_src, own_dst):
        @pl.loop(1, m_all)
        def _(step):
            other = member(step)
            remote(
                src_of(other), dst, plane_send.at[kind, c], plane_recv.at[kind, c], g, other
            ).start()

        pltpu.make_async_copy(own_src, own_dst, plane_own.at[kind, c]).start()

    def send_q(c):
        spread_out(0, c, lambda o: sq.at[c, o], rq.at[c, :, m], sq.at[c, m], rq.at[c, :, m])

    def send_kv(c):
        spread_out(
            1, c, lambda o: skv.at[c, o], rkv.at[c, :, :, m], skv.at[c, m], rkv.at[c, :, :, m]
        )

    def send_answers(c):
        spread_out(2, c, lambda o: sa.at[c, :, o], back.at[c, m], sa.at[c, :, m], back.at[c, m])

    def wait_q(c):
        wait_for(rq.at[c, :, pl.ds(0, m_all - 1)], plane_recv.at[0, c])
        wait_for(rq.at[c, :, m], plane_own.at[0, c])

    def wait_kv(c):
        wait_for(rkv.at[c, :, :, pl.ds(0, m_all - 1)], plane_recv.at[1, c])
        wait_for(rkv.at[c, :, :, m], plane_own.at[1, c])

    def wait_answers(c):
        wait_for(back.at[c, pl.ds(0, m_all - 1)], plane_recv.at[2, c])
        wait_for(back.at[c, m], plane_own.at[2, c])

    def pack(c):
        h, part = lax.div(c, p.parts), lax.rem(c, p.parts)
        columns = pl.ds(pl.multiple_of(h * LANES, LANES), LANES)
        data = jnp.concatenate([q_ref[:, columns], k_ref[:, columns], v_ref[:, columns]], axis=1)
        select = onehot(
            iota((p.crows, p.tokens), 0) + part * p.crows == key_ref[pl.ds(h, 1), :]
        )
        moved = dot(select, data).astype(BF16)
        shape = (m_all, p.rc, p.stride, LANES)
        sq[c] = moved[:, :LANES].reshape(shape)
        skv[c, :, 0] = moved[:, LANES : 2 * LANES].reshape(shape)
        skv[c, :, 1] = moved[:, 2 * LANES :].reshape(shape)

    def pack_wide():
        for h in range(heads):
            columns = slice(h * LANES, (h + 1) * LANES)
            data = jnp.concatenate(
                [q_ref[:, columns], k_ref[:, columns], v_ref[:, columns]], axis=1
            )
            select = onehot(iota((p.wide, p.tokens), 0) == wide_ref[h : h + 1, :])
            moved = dot(select, data).astype(BF16)
            for i in range(3):
                swb[h, i] = moved[:, i * LANES : (i + 1) * LANES]
            target = h * p.spread

            @pl.when(m == target)
            def _():
                pltpu.make_async_copy(swb.at[h], rwb.at[:, m], one_own.at[0]).start()

            @pl.when(m != target)
            def _():
                remote(
                    swb.at[h], rwb.at[:, m], one_send.at[0], one_recv.at[0], g, target
                ).start()

    def wait_wide():
        wait_for(rwb.at[:, pl.ds(0, m_all - 1)], one_recv.at[0])
        wait_for(rwb.at[:, m], one_own.at[0])

    def send_labels():
        make_labels(p, ids_ref, wide_ref, place_ref, slab)

        @pl.loop(1, m_all)
        def _(step):
            other = member(step)
            remote(slab.at[other], rlab.at[m], one_send.at[1], one_recv.at[1], g, other).start()

        pltpu.make_async_copy(slab.at[m], rlab.at[m], one_own.at[1]).start()

    def share_labels():
        wait_for(rlab.at[pl.ds(0, m_all - 1)], one_recv.at[1])
        wait_for(rlab.at[m], one_own.at[1])
        mine = read_labels(p, rlab)
        tabf[g] = mine
        tab[g] = mine.astype(BF16)
        for c, holding in enumerate(p.holders):

            @pl.when(g > holding)
            def _():
                remote(tab.at[g], tab.at[g], tab_send.at[c], tab_recv.at[g], holding, m).start()

        @pl.when(lifts)
        def _():
            remote(
                tab.at[g], tab.at[g], tab_send.at[len(p.holders)], tab_recv.at[g], g + 1, m
            ).start()

    def fetch_labels():
        def fetch(s):
            wait_for(tab.at[s], tab_recv.at[s])
            tabf[s] = tab[s].astype(F32)

        @pl.when(pair_holder)
        def _():
            fetch(g - 1)

        @pl.loop(0, n_sets)
        def _(i):
            fetch(g + 1 + i)

    def forward(c):
        for i, holding in enumerate(p.holders):

            @pl.when(g > holding)
            def _():
                s = g - holding - 1
                remote(
                    rq.at[c], zq.at[s, c], down_send.at[i, c], down_recv.at[s, c], holding, m
                ).start()

    def lift(c):
        @pl.when(lifts)
        def _():
            remote(rkv.at[c], zkv.at[c], up_send.at[c], up_recv.at[c], g + 1, m).start()

    def forward_wide():
        @pl.when(is_wide)
        def _():
            wait_wide()
            for i, holding in enumerate(p.holders):

                @pl.when(g > holding)
                def _():
                    s = g - holding - 1
                    remote(
                        rwb.at[0], zwq.at[s], down_send.at[i, chunks],
                        down_recv.at[s, chunks], holding, m,
                    ).start()

            @pl.when(lifts)
            def _():
                remote(
                    rwb.at[pl.ds(1, 2)], zwkv, up_send.at[chunks], up_recv.at[chunks], g + 1, m
                ).start()

    def tables(s, h):
        return tabf[s, pl.ds(pl.multiple_of(h * m_all, m_all), m_all), :]

    def flat(value):
        return value.reshape(-1, LANES)

    def causal(size, keys, first):
        return iota((size, keys), 1) <= iota((size, keys), 0) + first

    def return_part(pin_ref, pinst_ref, src, st, s, slot):
        target = g + 1 + s
        where = jnp.where(last_holder, p.psets - 1, lax.div(g - 1, 2))
        remote(
            src, pin_ref(where), ret_send.at[0, s, slot], ret_recv.at[0, where, slot], target, m
        ).start()
        remote(
            st, pinst_ref(where), ret_send.at[1, s, slot], ret_recv.at[1, where, slot], target, m
        ).start()

    def tile_of(c):
        return lax.div(c, p.parts), lax.rem(c, p.parts) * p.rc

    def own_part(c, with_before):
        h, r = tile_of(c)
        for j in range(p.rc):
            offset = (r + j) * p.stride
            table = tables(g, h)
            lq, lk = row_labels(table, p.stride, offset), lane_labels(table, p.stride, offset)
            ok = (lq == lk) & causal(p.rows, p.rows, 0)
            parts = [(flat(rkv[c, 0, j]), flat(rkv[c, 1, j]), ok)]
            if with_before:
                before = lane_labels(tables(g - 1, h), p.stride, offset)
                parts.append((flat(zkv[c, 0, j]), flat(zkv[c, 1, j]), lq == before))
            out, lse = attend(flat(rq[c, j]), parts)

            @pl.when(n_ret == 0)
            def _():
                sa[c, j] = out.astype(BF16).reshape(m_all, p.stride, LANES)

            @pl.when(n_ret > 0)
            def _():
                loc[c, j] = out
                count = p.rows // LANES
                locst[c, j * count : (j + 1) * count, :] = to_rows(lse)

        @pl.when(n_ret == 0)
        def _():
            send_answers(c)

    def visitors(c, with_before):
        h, r = tile_of(c)

        @pl.loop(0, n_sets)
        def _(s):
            wait_for(zq.at[s, c], down_recv.at[s, c])
            for j in range(p.rc):
                offset = (r + j) * p.stride
                lq = row_labels(tables(g + 1 + s, h), p.stride, offset)
                lk = lane_labels(tables(g, h), p.stride, offset)
                parts = [(flat(rkv[c, 0, j]), flat(rkv[c, 1, j]), lq == lk)]
                if with_before:
                    before = lane_labels(tables(g - 1, h), p.stride, offset)
                    parts.append((flat(zkv[c, 0, j]), flat(zkv[c, 1, j]), lq == before))
                out, lse = attend(flat(zq[s, c, j]), parts)
                zq[s, c, j] = out.astype(BF16).reshape(m_all, p.stride, LANES)
                count = p.rows // LANES
                pst[s, c, j * count : (j + 1) * count, :] = to_rows(lse)
            return_part(
                lambda w: pin.at[w, c], lambda w: pinst.at[w, c], zq.at[s, c], pst.at[s, c], s, c
            )

    def wide_blocks():
        size = math.gcd(BLOCK, p.wrows)
        return size, range(0, p.wrows, size)

    def own_wide(with_before):
        size, starts = wide_blocks()
        table = tables(g, heads)
        lq_all, lk_all = row_labels(table, p.wide, 0), lane_labels(table, p.wide, 0)
        queries = flat(rwb[0])
        keys, values = flat(rwb[1]), flat(rwb[2])
        outs, lses = [], []
        for first in starts:
            lq = lq_all[first : first + size]
            end = first + size
            ok = (lq == lk_all[:, :end]) & causal(size, end, first)
            parts = [(keys[:end], values[:end], ok)]
            if with_before:
                before = lane_labels(tables(g - 1, heads), p.wide, 0)
                parts.append((flat(zwkv[0]), flat(zwkv[1]), lq == before))
            out, lse = attend(queries[first:end], parts)
            outs.append(out)
            lses.append(to_rows(lse))
        out = jnp.concatenate(outs, axis=0)

        @pl.when(n_ret == 0)
        def _():
            swa[...] = out.astype(BF16).reshape(m_all, p.wide, LANES)
            send_wide()

        @pl.when(n_ret > 0)
        def _():
            wloc[...] = out
            wlocst[0 : p.wrows // LANES, :] = jnp.concatenate(lses, axis=0)

    def visitors_wide(with_before):
        size, starts = wide_blocks()

        @pl.loop(0, n_sets)
        def _(s):
            wait_for(zwq.at[s], down_recv.at[s, chunks])
            lq_all = row_labels(tables(g + 1 + s, heads), p.wide, 0)
            lk = lane_labels(tables(g, heads), p.wide, 0)
            queries = flat(zwq[s])
            outs, lses = [], []
            for first in starts:
                lq = lq_all[first : first + size]
                parts = [(flat(rwb[1]), flat(rwb[2]), lq == lk)]
                if with_before:
                    before = lane_labels(tables(g - 1, heads), p.wide, 0)
                    parts.append((flat(zwkv[0]), flat(zwkv[1]), lq == before))
                out, lse = attend(queries[first : first + size], parts)
                outs.append(out.astype(BF16))
                lses.append(to_rows(lse))
            zwq[s] = jnp.concatenate(outs, axis=0).reshape(m_all, p.wide, LANES)
            wst[s, 0 : p.wrows // LANES, :] = jnp.concatenate(lses, axis=0)
            return_part(
                lambda w: wpin.at[w], lambda w: wpinst.at[w], zwq.at[s], wst.at[s], s, chunks
            )

    def send_wide():
        @pl.loop(1, m_all)
        def _(step):
            other = member(step)
            remote(
                swa.at[other], wback.at[head_of], one_send.at[2], one_recv.at[2], g, other
            ).start()

        pltpu.make_async_copy(swa.at[m], wback.at[head_of], one_own.at[2]).start()

    def merge(outs, lses):
        top = functools.reduce(jnp.maximum, lses)
        weights = [jnp.exp2(x - top) for x in lses]
        share = 1.0 / sum(weights)
        weights = [w * share for w in weights]
        blocks = []
        for i in range(weights[0].shape[0]):
            rows = slice(i * LANES, (i + 1) * LANES)
            blocks.append(sum(to_columns(w[i : i + 1]) * o[rows] for w, o in zip(weights, outs)))
        return jnp.concatenate(blocks, axis=0).astype(BF16)

    def combine(c):
        for k in range(1, p.psets + 1):

            @pl.when(n_ret == k)
            def _():
                for i in range(k):
                    wait_for(pin.at[i, c], ret_recv.at[0, i, c])
                    wait_for(pinst.at[i, c], ret_recv.at[1, i, c])
                count = p.rows // LANES
                for j in range(p.rc):
                    rows = slice(j * count, (j + 1) * count)
                    outs = [loc[c, j]] + [flat(pin[i, c, j]) for i in range(k)]
                    lses = [locst[c, rows, :]] + [pinst[i, c, rows, :] for i in range(k)]
                    sa[c, j] = merge(outs, lses).reshape(m_all, p.stride, LANES)

        send_answers(c)

    def combine_wide():
        for k in range(1, p.psets + 1):

            @pl.when(n_ret == k)
            def _():
                for i in range(k):
                    wait_for(wpin.at[i], ret_recv.at[0, i, chunks])
                    wait_for(wpinst.at[i], ret_recv.at[1, i, chunks])
                count = p.wrows // LANES
                outs = [wloc[...]] + [flat(wpin[i]) for i in range(k)]
                lses = [wlocst[:count, :]] + [wpinst[i, :count, :] for i in range(k)]
                swa[...] = merge(outs, lses).reshape(m_all, p.wide, LANES)

        send_wide()

    def make_columns():
        for h in range(heads):
            line = jnp.broadcast_to(key_ref[h : h + 1, :].astype(F32), (LANES, p.tokens))
            kcol_ref[h] = jnp.transpose(line).astype(jnp.int32)

    def pick(h, first, count):
        pieces = []
        for at in range(0, count, LANES):
            width = min(LANES, count - at)
            lane = iota((p.tokens, width), 1) + (first + at)
            pieces.append(onehot(lane == kcol_ref[h, :, :width]))
        return jnp.concatenate(pieces, axis=1)

    def unpack(c):
        wait_answers(c)
        h, part = lax.div(c, p.parts), lax.rem(c, p.parts)
        columns = pl.ds(pl.multiple_of(h * LANES, LANES), LANES)
        rows = dot(pick(h, part * p.crows, p.crows), flat(back[c])).astype(BF16)

        @pl.when(part == 0)
        def _():
            out_ref[:, columns] = rows

        @pl.when(part > 0)
        def _():
            out_ref[:, columns] = out_ref[:, columns] + rows

    def unpack_wide():
        @pl.when(is_wide)
        def _():
            wait_for(wback.at[pl.ds(0, heads - 1)], one_recv.at[2])
            wait_for(wback.at[head_of], one_own.at[2])

        @pl.when(jnp.logical_not(is_wide))
        def _():
            wait_for(wback, one_recv.at[2])

        for h in range(heads):
            columns = slice(h * LANES, (h + 1) * LANES)
            rows = dot(pick(h, p.base, p.wide), wback[h]).astype(BF16)
            out_ref[:, columns] = out_ref[:, columns] + rows

    place_tokens(p, ids_ref, key_ref, wide_ref, place_ref)
    pl.semaphore_wait(barrier, m_all - 1 + p.groups - 1)

    wide_at, lag, behind = 2, 4, 1

    downs = (g >= 2) & jnp.logical_not(lifts | pair_holder)

    def pass_on(c):
        @pl.when(downs)
        def _():
            wait_q(c)
            forward(c)

        @pl.when(lifts)
        def _():
            wait_kv(c)
            lift(c)

    send_labels()

    @pl.loop(0, chunks)
    def _(c):
        pack(c)

        @pl.when(jnp.logical_not(lifts))
        def _():
            send_q(c)

        @pl.when(jnp.logical_not(downs))
        def _():
            send_kv(c)

        @pl.when(c == 1)
        def _():
            pack_wide()

        @pl.when(c == 1)
        def _():
            share_labels()

        @pl.when(c >= behind)
        def _():
            pass_on(c - behind)

        @pl.when((c == 3) & jnp.logical_not(pair_holder))
        def _():
            forward_wide()

    @pl.when(lifts)
    def _():
        @pl.loop(0, chunks)
        def _(c):
            send_q(c)

    @pl.when(downs)
    def _():
        @pl.loop(0, chunks)
        def _(c):
            send_kv(c)

    @pl.loop(chunks - behind, chunks)
    def _(c):
        pass_on(c)

    make_columns()

    @pl.when(pair_holder)
    def _():
        @pl.loop(0, chunks)
        def _(c):
            wait_q(c)
            forward(c)
            wait_kv(c)

            @pl.when(c == 0)
            def _():
                fetch_labels()

            @pl.when(c == 1)
            def _():
                forward_wide()

            wait_for(zkv.at[c], up_recv.at[c])
            visitors(c, True)
            own_part(c, True)

            @pl.when((c == wide_at) & is_wide)
            def _():
                wait_for(zwkv, up_recv.at[chunks])
                visitors_wide(True)
                own_wide(True)

            @pl.when((n_ret == 0) & (c >= lag))
            def _():
                unpack(c - lag)

    @pl.when(jnp.logical_not(pair_holder))
    def _():
        @pl.when(last_holder)
        def _():
            fetch_labels()

        @pl.loop(0, chunks)
        def _(c):
            @pl.when(lifts)
            def _():
                wait_q(c)
                forward(c)

            @pl.when(downs)
            def _():
                wait_kv(c)

            own_part(c, False)

            @pl.when(last_holder)
            def _():
                visitors(c, False)

            @pl.when((c == wide_at) & is_wide)
            def _():
                own_wide(False)

                @pl.when(last_holder)
                def _():
                    visitors_wide(False)

            @pl.when((n_ret == 0) & (c >= lag))
            def _():
                unpack(c - lag)

    @pl.when(n_ret == 0)
    def _():
        @pl.loop(chunks - lag, chunks - 1)
        def _(c):
            unpack(c)

    @pl.when(n_ret > 0)
    def _():
        @pl.loop(0, chunks)
        def _(c):
            combine(c)

            @pl.when((c == wide_at) & is_wide)
            def _():
                combine_wide()

            @pl.when(c > 0)
            def _():
                unpack(c - 1)

    unpack_wide()
    unpack(chunks - 1)

    @pl.loop(0, chunks)
    def _(c):
        wait_for(sq.at[c, pl.ds(0, m_all - 1)], plane_send.at[0, c])
        wait_for(skv.at[c, pl.ds(0, m_all - 1)], plane_send.at[1, c])
        wait_for(sa.at[c, :, pl.ds(0, m_all - 1)], plane_send.at[2, c])
        for i, holding in enumerate(p.holders):

            @pl.when(g > holding)
            def _():
                wait_for(rq.at[c], down_send.at[i, c])

        @pl.when(lifts)
        def _():
            wait_for(rkv.at[c], up_send.at[c])

        @pl.loop(0, n_sets)
        def _(s):
            wait_for(zq.at[s, c], ret_send.at[0, s, c])
            wait_for(pst.at[s, c], ret_send.at[1, s, c])

    for i, holding in enumerate(p.holders):

        @pl.when(g > holding)
        def _():
            wait_for(tab.at[g], tab_send.at[i])

    @pl.when(lifts)
    def _():
        wait_for(tab.at[g], tab_send.at[len(p.holders)])

    wait_for(slab.at[pl.ds(0, m_all - 1)], one_send.at[1])

    @pl.when(jnp.logical_not(is_wide))
    def _():
        wait_for(swb, one_send.at[0])

    @pl.when(is_wide)
    def _():
        wait_for(swb.at[pl.ds(0, heads - 1)], one_send.at[0])
        wait_for(swa.at[pl.ds(0, m_all - 1)], one_send.at[2])
        for i, holding in enumerate(p.holders):

            @pl.when(g > holding)
            def _():
                wait_for(rwb.at[0], down_send.at[i, chunks])

        @pl.when(lifts)
        def _():
            wait_for(zwkv, up_send.at[chunks])

        @pl.loop(0, n_sets)
        def _(s):
            wait_for(zwq.at[s], ret_send.at[0, s, chunks])
            wait_for(wst.at[s], ret_send.at[1, s, chunks])


VMEM_SPEC = pl.BlockSpec(memory_space=pltpu.VMEM)


def local(query_rows, key_rows, value_rows, cluster_ids):
    groups, members = lax.axis_size("grp"), lax.axis_size("ctx")
    heads, tokens = cluster_ids.shape
    p = Plan(groups, members, heads, tokens)
    c, rc, m, st, w = p.chunks, p.rc, p.members, p.stride, p.wide
    qs, ps, hold = p.qsets, p.psets, len(p.holders)
    assert rc * p.rows // LANES <= 8 and p.wrows // LANES <= 8 and p.ranges * st <= LANES

    def half(*shape):
        return pltpu.VMEM((*shape, LANES), BF16)

    def full(*shape):
        return pltpu.VMEM((*shape, LANES), F32)

    ids = pltpu.VMEM((up(heads, 8), tokens), jnp.int32)
    dma = pltpu.SemaphoreType.DMA
    return pl.pallas_call(
        functools.partial(kernel, p),
        out_shape=jax.ShapeDtypeStruct((tokens, heads * LANES), BF16),
        in_specs=[VMEM_SPEC] * 4,
        out_specs=VMEM_SPEC,
        scratch_shapes=[
            ids, ids, ids, pltpu.VMEM((heads, tokens, LANES), jnp.int32),
            half(c, m, rc, st), half(c, m, 2, rc, st), half(heads, 3, w), half(m, SUB),
            half(c, rc, m, st), half(c, 2, rc, m, st), half(3, m, w), half(m, SUB),
            half(groups, p.table), full(groups, p.table),
            half(qs, c, rc, m, st), half(qs, m, w), half(c, 2, rc, m, st), half(2, m, w),
            full(qs, c, 8), full(qs, 8),
            half(ps, c, rc, m, st), half(ps, m, w), full(ps, c, 8), full(ps, 8),
            full(c, rc, p.rows), full(c, 8), full(p.wrows), full(8),
            half(c, m, rc, st), half(heads, w),
            dma((3, c)), dma((3, c)), dma((3, c)), dma((3,)), dma((3,)), dma((3,)),
            dma((c + 1,)), dma((c + 1,)), dma((hold, c + 1)), dma((qs, c + 1)),
            dma((2, qs, c + 1)), dma((2, ps, c + 1)), dma((hold + 1,)), dma((groups,)),
        ],
        compiler_params=pltpu.CompilerParams(
            collective_id=0, has_side_effects=True, vmem_limit_bytes=60 * 2**20
        ),
    )(cluster_ids, query_rows, key_rows, value_rows)


def solution(mesh):
    return jax.shard_map(
        local,
        mesh=mesh,
        in_specs=(
            P(("grp", "ctx"), None),
            P(("grp", "ctx"), None),
            P(("grp", "ctx"), None),
            P(None, ("grp", "ctx")),
        ),
        out_specs=P(("grp", "ctx"), None),
        check_vma=False,
    )
```

```python
import functools
import itertools
import math

import jax
import jax.numpy as jnp
from jax import lax
from jax.experimental import pallas as pl
from jax.experimental.pallas import tpu as pltpu
from jax.sharding import PartitionSpec as P

CL_SHIFT = 3
LANES = 128
SUB = 16
BLOCK = 256
NEG_FILL = -1e30
F32 = jnp.float32
BF16 = jnp.bfloat16
FACTOR = LANES**-0.5 * math.log2(math.e)
MESH = pl.DeviceIdType.MESH


def up(value, step):
    return (value + step - 1) // step * step


def shift_of(value):
    assert value & (value - 1) == 0
    return value.bit_length() - 1


class Plan:
    def __init__(self, groups, members, heads, tokens):
        self.groups, self.members, self.heads, self.tokens = groups, members, heads, tokens
        self.n = groups * members
        self.cap = tokens // self.n
        self.busy = 3 * tokens // self.n
        self.stride = up(self.cap, SUB)
        self.wide = up(self.busy, SUB)
        self.ranges = groups
        self.parts = 2
        self.rc = self.ranges // self.parts
        self.chunks = heads * self.parts
        self.rows = members * self.stride
        self.mrows = self.rc * self.stride
        self.crows = members * self.mrows
        self.srows = self.rc * self.rows // LANES
        self.wrows = members * self.wide
        self.base = self.n * self.stride
        self.spread = members // heads
        self.table = up((heads + 1) * members, SUB)
        self.holders = [c for c in range(1, groups - 2, 2)] + [groups - 2]
        self.qsets = groups - 2
        self.psets = groups // 2


def iota(shape, dim):
    return lax.broadcasted_iota(jnp.int32, shape, dim)


def dot(a, b):
    return jnp.dot(a, b, preferred_element_type=F32)


def dot_t(a, b):
    return lax.dot_general(a, b, (((1,), (1,)), ((), ())), preferred_element_type=F32)


def onehot(cond):
    return jnp.where(cond, 1.0, 0.0).astype(BF16)


def place_tokens(p, ids_ref, key_ref, wide_ref, place_ref):
    n, t = p.n, p.tokens
    blk = math.gcd(BLOCK, t)
    earlier = onehot(iota((blk, blk), 0) < iota((blk, blk), 1))
    owners, members = [], []
    for h in range(p.heads):
        owner = lax.shift_right_logical(ids_ref[h : h + 1, :], CL_SHIFT)
        owners.append(owner)
        members.append(jnp.where(iota((n, t), 0) == owner, 1.0, 0.0))
    member = jnp.concatenate(members, axis=0)
    carry = jnp.zeros((p.heads * n, 1), F32)
    slots = []
    for b in range(0, t, blk):
        piece = member[:, b : b + blk]
        slots.append(piece * (dot(piece.astype(BF16), earlier) + carry))
        carry += jnp.sum(piece, axis=1, keepdims=True)
    slot_all = jnp.concatenate(slots, axis=1)
    full = jnp.where(carry > p.cap, 1.0, 0.0)
    for h in range(p.heads):
        rows = slice(h * n, (h + 1) * n)
        owner = owners[h]
        slot = jnp.sum(slot_all[rows], axis=0, keepdims=True).astype(jnp.int32)
        is_busy = jnp.sum(members[h] * full[rows], axis=0, keepdims=True) > 0.5
        who = lax.shift_right_logical(owner, shift_of(p.ranges))
        which = owner & (p.ranges - 1)
        part = lax.shift_right_logical(which, shift_of(p.rc))
        row = part * p.crows + who * p.mrows + (which & (p.rc - 1)) * p.stride + slot
        key_ref[h : h + 1, :] = jnp.where(is_busy, p.base + slot, row)
        wide_ref[h : h + 1, :] = jnp.where(is_busy, slot, -1)
        place_ref[h : h + 1, :] = jnp.where(is_busy, -1, which * p.stride + slot)


def make_labels(p, ids_ref, wide_ref, place_ref, slab_ref):
    m, t = p.members, p.tokens
    row = iota((m * SUB, m), 0) - iota((m * SUB, m), 1) * SUB
    spread = jnp.zeros((m * SUB, LANES), F32)
    for h in range(p.heads):
        ids = ids_ref[h : h + 1, :]
        who = lax.shift_right_logical(ids, CL_SHIFT + shift_of(p.ranges))
        label = ((ids & (2**CL_SHIFT - 1)) + 1).astype(F32)
        mine = jnp.where(iota((m, t), 0) == who, label, 0.0).astype(BF16)
        spot = onehot(iota((LANES, t), 0) == place_ref[h : h + 1, :])
        spread += dot(onehot(row == h), dot_t(mine, spot).astype(BF16))
        spot = onehot(iota((LANES, t), 0) == wide_ref[h : h + 1, :])
        line = dot_t(jnp.broadcast_to(label, (m, t)).astype(BF16), spot)
        line = jnp.where(iota((m, LANES), 0) == h * p.spread, line, 0.0)
        spread += dot(onehot(row == p.heads), line.astype(BF16))
    slab_ref[...] = spread.astype(BF16).reshape(m, SUB, LANES)


def read_labels(p, rlab_ref):
    m = p.members
    total = m * SUB
    want = iota((p.table, total), 0)
    src, h = want & (m - 1), lax.shift_right_logical(want, shift_of(m))
    pick = onehot((iota((p.table, total), 1) == src * SUB + h) & (h <= p.heads))
    return dot(pick, rlab_ref[...].reshape(total, LANES))


def row_labels(table, width, offset):
    m = table.shape[0]
    total = m * width
    src = iota((m, width, m), 0).reshape(total, m)
    spread = dot(onehot(src == iota((total, m), 1)), table.astype(BF16))
    lane = iota((m, width, LANES), 1).reshape(total, LANES) + offset
    return jnp.sum(
        jnp.where(iota((total, LANES), 1) == lane, spread, 0.0), axis=1, keepdims=True
    )


def lane_labels(table, width, offset):
    m = table.shape[0]
    total = m * width
    lane = iota((1, total), 1)
    src = jnp.floor((lane.astype(F32) + 0.5) * (1.0 / width)).astype(jnp.int32)
    spot = onehot(iota((LANES, total), 0) == lane - src * width + offset)
    spread = dot(table.astype(BF16), spot)
    return jnp.sum(jnp.where(iota((m, total), 0) == src, spread, 0.0), axis=0, keepdims=True)


def attend(queries, parts):
    masked = [jnp.where(ok, dot_t(queries, k), NEG_FILL) for k, _, ok in parts]
    top = functools.reduce(jnp.maximum, [jnp.max(s, axis=1, keepdims=True) for s in masked])
    weights = [jnp.exp2((s - top) * FACTOR) for s in masked]
    total = sum(jnp.sum(w, axis=1, keepdims=True) for w in weights)
    acc = sum(dot(w.astype(BF16), v) for w, (_, v, _) in zip(weights, parts))
    return acc * (1.0 / total), top * FACTOR + jnp.log2(total)


def to_rows(column):
    count = column.shape[0] // LANES
    wide = jnp.broadcast_to(column, (column.shape[0], LANES)).reshape(count, LANES, LANES)
    eye = iota((count, LANES, LANES), 1) == iota((count, LANES, LANES), 2)
    return jnp.sum(jnp.where(eye, wide, 0.0), axis=1)


def to_columns(row):
    return jnp.transpose(jnp.broadcast_to(row, (LANES, LANES)))


def kernel(
    p, ids_ref, q_hbm, k_hbm, v_hbm, out_ref, q_ref, k_ref, v_ref,
    key_ref, wide_ref, place_ref, kcol_ref,
    sq, skv, swb, slab, rq, rkv, rwb, rlab, tab, tabf,
    zq, zwq, zkv, zwkv, pst, wst, pin, wpin, pinst, wpinst,
    loc, locst, wloc, wlocst, back, wback,
    load_sem, plane_send, plane_recv, plane_own, one_send, one_recv, one_own,
    up_send, up_recv, down_send, down_recv, ret_send, ret_recv, tab_send, tab_recv,
):
    m_all, heads, chunks = p.members, p.heads, p.chunks
    g, m = lax.axis_index("grp"), lax.axis_index("ctx")
    pair_holder = (g < p.groups - 2) & (lax.rem(g, 2) == 1)
    last_holder = g == p.groups - 2
    holder = pair_holder | last_holder
    lifts = (g < p.groups - 2) & (lax.rem(g, 2) == 0)
    n_sets = jnp.where(holder, p.groups - 1 - g, 0)
    n_ret = lax.div(jnp.minimum(g, p.groups - 2), 2) + jnp.where(g == p.groups - 1, 1, 0)
    is_wide = lax.rem(m, p.spread) == 0
    sa, swa = pin.at[0], wpin.at[0]
    head_of = lax.div(m, p.spread)
    last = chunks * p.rc

    def member(step):
        return lax.rem(m + step, m_all)

    def remote(src, dst, send, recv, plane, who):
        return pltpu.make_async_remote_copy(
            src_ref=src, dst_ref=dst, send_sem=send, recv_sem=recv,
            device_id=(plane, who), device_id_type=MESH,
        )

    def wait_for(ref, sem):
        pltpu.make_async_copy(ref, ref, sem).wait()

    loads = [
        pltpu.make_async_copy(src, dst, load_sem.at[i])
        for i, (src, dst) in enumerate([(q_hbm, q_ref), (k_hbm, k_ref), (v_hbm, v_ref)])
    ]
    for load in loads:
        load.start()

    barrier = pltpu.get_barrier_semaphore()

    @pl.loop(1, m_all)
    def _(step):
        pl.semaphore_signal(barrier, inc=1, device_id=(g, member(step)), device_id_type=MESH)

    @pl.loop(1, p.groups)
    def _(step):
        pl.semaphore_signal(
            barrier, inc=1, device_id=(lax.rem(g + step, p.groups), m), device_id_type=MESH
        )

    def spread_out(kind, c, src_of, dst, own_src, own_dst):
        @pl.loop(1, m_all)
        def _(step):
            other = member(step)
            remote(
                src_of(other), dst, plane_send.at[kind, c], plane_recv.at[kind, c], g, other
            ).start()

        pltpu.make_async_copy(own_src, own_dst, plane_own.at[kind, c]).start()

    def send_q(c):
        spread_out(0, c, lambda o: sq.at[c, o], rq.at[c, :, m], sq.at[c, m], rq.at[c, :, m])

    def send_kv(c):
        spread_out(
            1, c, lambda o: skv.at[c, o], rkv.at[c, :, :, m], skv.at[c, m], rkv.at[c, :, :, m]
        )

    def send_answers(c):
        spread_out(2, c, lambda o: sa.at[c, :, o], back.at[c, m], sa.at[c, :, m], back.at[c, m])

    def wait_q(c):
        wait_for(rq.at[c, :, pl.ds(0, m_all - 1)], plane_recv.at[0, c])
        wait_for(rq.at[c, :, m], plane_own.at[0, c])

    def wait_kv(c):
        wait_for(rkv.at[c, :, :, pl.ds(0, m_all - 1)], plane_recv.at[1, c])
        wait_for(rkv.at[c, :, :, m], plane_own.at[1, c])

    def wait_answers(c):
        wait_for(back.at[c, pl.ds(0, m_all - 1)], plane_recv.at[2, c])
        wait_for(back.at[c, m], plane_own.at[2, c])

    def pack(c):
        h, part = lax.div(c, p.parts), lax.rem(c, p.parts)
        columns = pl.ds(pl.multiple_of(h * LANES, LANES), LANES)
        data = jnp.concatenate([q_ref[:, columns], k_ref[:, columns], v_ref[:, columns]], axis=1)
        select = onehot(
            iota((p.crows, p.tokens), 0) + part * p.crows == key_ref[pl.ds(h, 1), :]
        )
        moved = dot(select, data).astype(BF16)
        shape = (m_all, p.rc, p.stride, LANES)
        sq[c] = moved[:, :LANES].reshape(shape)
        skv[c, :, 0] = moved[:, LANES : 2 * LANES].reshape(shape)
        skv[c, :, 1] = moved[:, 2 * LANES :].reshape(shape)

    def pack_wide():
        for h in range(heads):
            columns = slice(h * LANES, (h + 1) * LANES)
            data = jnp.concatenate(
                [q_ref[:, columns], k_ref[:, columns], v_ref[:, columns]], axis=1
            )
            select = onehot(iota((p.wide, p.tokens), 0) == wide_ref[h : h + 1, :])
            moved = dot(select, data).astype(BF16)
            for i in range(3):
                swb[h, i] = moved[:, i * LANES : (i + 1) * LANES]
            target = h * p.spread

            @pl.when(m == target)
            def _():
                pltpu.make_async_copy(swb.at[h], rwb.at[:, m], one_own.at[0]).start()

            @pl.when(m != target)
            def _():
                remote(
                    swb.at[h], rwb.at[:, m], one_send.at[0], one_recv.at[0], g, target
                ).start()

    def wait_wide():
        wait_for(rwb.at[:, pl.ds(0, m_all - 1)], one_recv.at[0])
        wait_for(rwb.at[:, m], one_own.at[0])

    def send_labels():
        @pl.loop(1, m_all)
        def _(step):
            other = member(step)
            remote(slab.at[other], rlab.at[m], one_send.at[1], one_recv.at[1], g, other).start()

        pltpu.make_async_copy(slab.at[m], rlab.at[m], one_own.at[1]).start()

    def share_labels():
        wait_for(rlab.at[pl.ds(0, m_all - 1)], one_recv.at[1])
        wait_for(rlab.at[m], one_own.at[1])
        mine = read_labels(p, rlab)
        tabf[g] = mine
        tab[g] = mine.astype(BF16)
        for c, holding in enumerate(p.holders):

            @pl.when(g > holding)
            def _():
                remote(tab.at[g], tab.at[g], tab_send.at[c], tab_recv.at[g], holding, m).start()

        @pl.when(lifts)
        def _():
            remote(
                tab.at[g], tab.at[g], tab_send.at[len(p.holders)], tab_recv.at[g], g + 1, m
            ).start()

    def fetch_labels():
        def fetch(s):
            wait_for(tab.at[s], tab_recv.at[s])
            tabf[s] = tab[s].astype(F32)

        @pl.when(pair_holder)
        def _():
            fetch(g - 1)

        @pl.loop(0, n_sets)
        def _(i):
            fetch(g + 1 + i)

    def forward(c):
        for j, (i, holding) in itertools.product(range(p.rc), enumerate(p.holders)):

            @pl.when(g > holding)
            def _():
                s = g - holding - 1
                remote(
                    rq.at[c, j], zq.at[s, c, j], down_send.at[i, c],
                    down_recv.at[s, c * p.rc + j], holding, m,
                ).start()

    def lift(c):
        @pl.when(lifts)
        def _():
            for j in range(p.rc):
                remote(
                    rkv.at[c, :, j], zkv.at[c, :, j], up_send.at[c],
                    up_recv.at[c * p.rc + j], g + 1, m,
                ).start()

    def forward_wide():
        @pl.when(is_wide)
        def _():
            wait_wide()
            for i, holding in enumerate(p.holders):

                @pl.when(g > holding)
                def _():
                    s = g - holding - 1
                    remote(
                        rwb.at[0], zwq.at[s], down_send.at[i, chunks],
                        down_recv.at[s, last], holding, m,
                    ).start()

            @pl.when(lifts)
            def _():
                remote(
                    rwb.at[pl.ds(1, 2)], zwkv, up_send.at[chunks], up_recv.at[last], g + 1, m
                ).start()

    def tables(s, h):
        return tabf[s, pl.ds(pl.multiple_of(h * m_all, m_all), m_all), :]

    def flat(value):
        return value.reshape(-1, LANES)

    def causal(size, keys, first):
        return iota((size, keys), 1) <= iota((size, keys), 0) + first

    def give_back(src, dst_of, kind, s, sent, slot):
        where = jnp.where(last_holder, p.psets - 1, lax.div(g - 1, 2))
        remote(
            src, dst_of(where), ret_send.at[kind, s, sent], ret_recv.at[kind, where, slot],
            g + 1 + s, m,
        ).start()

    def tile_of(c):
        return lax.div(c, p.parts), lax.rem(c, p.parts) * p.rc

    def own_part(c, with_before):
        h, r = tile_of(c)
        for j in range(p.rc):
            offset = (r + j) * p.stride
            table = tables(g, h)
            lq, lk = row_labels(table, p.stride, offset), lane_labels(table, p.stride, offset)
            ok = (lq == lk) & causal(p.rows, p.rows, 0)
            parts = [(flat(rkv[c, 0, j]), flat(rkv[c, 1, j]), ok)]
            if with_before:
                before = lane_labels(tables(g - 1, h), p.stride, offset)
                parts.append((flat(zkv[c, 0, j]), flat(zkv[c, 1, j]), lq == before))
            out, lse = attend(flat(rq[c, j]), parts)

            @pl.when(n_ret == 0)
            def _():
                sa[c, j] = out.astype(BF16).reshape(m_all, p.stride, LANES)

            @pl.when(n_ret > 0)
            def _():
                loc[c, j] = out
                count = p.rows // LANES
                locst[c, j * count : (j + 1) * count, :] = to_rows(lse)

        @pl.when(n_ret == 0)
        def _():
            send_answers(c)

    def visitors(c, with_before):
        h, r = tile_of(c)
        count = p.rows // LANES
        for j in range(p.rc):
            offset = (r + j) * p.stride
            slot = c * p.rc + j
            if with_before:
                wait_for(zkv.at[c, :, j], up_recv.at[slot])

            @pl.loop(0, n_sets)
            def _(s):
                wait_for(zq.at[s, c, j], down_recv.at[s, slot])
                lq = row_labels(tables(g + 1 + s, h), p.stride, offset)
                lk = lane_labels(tables(g, h), p.stride, offset)
                parts = [(flat(rkv[c, 0, j]), flat(rkv[c, 1, j]), lq == lk)]
                if with_before:
                    before = lane_labels(tables(g - 1, h), p.stride, offset)
                    parts.append((flat(zkv[c, 0, j]), flat(zkv[c, 1, j]), lq == before))
                out, lse = attend(flat(zq[s, c, j]), parts)
                zq[s, c, j] = out.astype(BF16).reshape(m_all, p.stride, LANES)
                pst[s, c, j * count : (j + 1) * count, :] = to_rows(lse)
                give_back(zq.at[s, c, j], lambda w: pin.at[w, c, j], 0, s, c, slot)
                if j == p.rc - 1:
                    stats = pl.ds(0, p.srows)
                    give_back(
                        pst.at[s, c, stats], lambda w: pinst.at[w, c, stats], 1, s, c, c
                    )

    def wide_blocks():
        size = math.gcd(BLOCK, p.wrows)
        return size, range(0, p.wrows, size)

    def own_wide(with_before):
        size, starts = wide_blocks()
        table = tables(g, heads)
        lq_all, lk_all = row_labels(table, p.wide, 0), lane_labels(table, p.wide, 0)
        queries = flat(rwb[0])
        keys, values = flat(rwb[1]), flat(rwb[2])
        outs, lses = [], []
        for first in starts:
            lq = lq_all[first : first + size]
            end = first + size
            ok = (lq == lk_all[:, :end]) & causal(size, end, first)
            parts = [(keys[:end], values[:end], ok)]
            if with_before:
                before = lane_labels(tables(g - 1, heads), p.wide, 0)
                parts.append((flat(zwkv[0]), flat(zwkv[1]), lq == before))
            out, lse = attend(queries[first:end], parts)
            outs.append(out)
            lses.append(to_rows(lse))
        out = jnp.concatenate(outs, axis=0)

        @pl.when(n_ret == 0)
        def _():
            swa[...] = out.astype(BF16).reshape(m_all, p.wide, LANES)
            send_wide()

        @pl.when(n_ret > 0)
        def _():
            wloc[...] = out
            wlocst[0 : p.wrows // LANES, :] = jnp.concatenate(lses, axis=0)

    def visitors_wide(with_before):
        size, starts = wide_blocks()

        @pl.loop(0, n_sets)
        def _(s):
            wait_for(zwq.at[s], down_recv.at[s, last])
            lq_all = row_labels(tables(g + 1 + s, heads), p.wide, 0)
            lk = lane_labels(tables(g, heads), p.wide, 0)
            queries = flat(zwq[s])
            outs, lses = [], []
            for first in starts:
                lq = lq_all[first : first + size]
                parts = [(flat(rwb[1]), flat(rwb[2]), lq == lk)]
                if with_before:
                    before = lane_labels(tables(g - 1, heads), p.wide, 0)
                    parts.append((flat(zwkv[0]), flat(zwkv[1]), lq == before))
                out, lse = attend(queries[first : first + size], parts)
                outs.append(out.astype(BF16))
                lses.append(to_rows(lse))
            zwq[s] = jnp.concatenate(outs, axis=0).reshape(m_all, p.wide, LANES)
            wst[s, 0 : p.wrows // LANES, :] = jnp.concatenate(lses, axis=0)
            give_back(zwq.at[s], lambda w: wpin.at[w], 0, s, chunks, last)
            give_back(wst.at[s], lambda w: wpinst.at[w], 1, s, chunks, chunks)

    def send_wide():
        @pl.loop(1, m_all)
        def _(step):
            other = member(step)
            remote(
                swa.at[other], wback.at[head_of], one_send.at[2], one_recv.at[2], g, other
            ).start()

        pltpu.make_async_copy(swa.at[m], wback.at[head_of], one_own.at[2]).start()

    def merge(outs, lses):
        top = functools.reduce(jnp.maximum, lses)
        weights = [jnp.exp2(x - top) for x in lses]
        share = 1.0 / sum(weights)
        weights = [w * share for w in weights]
        blocks = []
        for i in range(weights[0].shape[0]):
            rows = slice(i * LANES, (i + 1) * LANES)
            blocks.append(sum(to_columns(w[i : i + 1]) * o[rows] for w, o in zip(weights, outs)))
        return jnp.concatenate(blocks, axis=0).astype(BF16)

    def combine(c):
        for k in range(1, p.psets + 1):

            @pl.when(n_ret == k)
            def _():
                for i in range(k):
                    wait_for(pinst.at[i, c, pl.ds(0, p.srows)], ret_recv.at[1, i, c])
                count = p.rows // LANES
                for j in range(p.rc):
                    for i in range(k):
                        wait_for(pin.at[i, c, j], ret_recv.at[0, i, c * p.rc + j])
                    rows = slice(j * count, (j + 1) * count)
                    outs = [loc[c, j]] + [flat(pin[i, c, j]) for i in range(k)]
                    lses = [locst[c, rows, :]] + [pinst[i, c, rows, :] for i in range(k)]
                    sa[c, j] = merge(outs, lses).reshape(m_all, p.stride, LANES)

        send_answers(c)

    def combine_wide():
        for k in range(1, p.psets + 1):

            @pl.when(n_ret == k)
            def _():
                for i in range(k):
                    wait_for(wpin.at[i], ret_recv.at[0, i, last])
                    wait_for(wpinst.at[i], ret_recv.at[1, i, chunks])
                count = p.wrows // LANES
                outs = [wloc[...]] + [flat(wpin[i]) for i in range(k)]
                lses = [wlocst[:count, :]] + [wpinst[i, :count, :] for i in range(k)]
                swa[...] = merge(outs, lses).reshape(m_all, p.wide, LANES)

        send_wide()

    def make_columns():
        for h in range(heads):
            line = jnp.broadcast_to(key_ref[h : h + 1, :].astype(F32), (LANES, p.tokens))
            kcol_ref[h] = jnp.transpose(line).astype(jnp.int32)

    def pick(h, first, count):
        pieces = []
        for at in range(0, count, LANES):
            width = min(LANES, count - at)
            lane = iota((p.tokens, width), 1) + (first + at)
            pieces.append(onehot(lane == kcol_ref[h, :, :width]))
        return jnp.concatenate(pieces, axis=1)

    def unpack(c):
        wait_answers(c)
        h, part = lax.div(c, p.parts), lax.rem(c, p.parts)
        columns = pl.ds(pl.multiple_of(h * LANES, LANES), LANES)
        rows = dot(pick(h, part * p.crows, p.crows), flat(back[c])).astype(BF16)

        @pl.when(part == 0)
        def _():
            out_ref[:, columns] = rows

        @pl.when(part > 0)
        def _():
            out_ref[:, columns] = out_ref[:, columns] + rows

    def unpack_wide():
        @pl.when(is_wide)
        def _():
            wait_for(wback.at[pl.ds(0, heads - 1)], one_recv.at[2])
            wait_for(wback.at[head_of], one_own.at[2])

        @pl.when(jnp.logical_not(is_wide))
        def _():
            wait_for(wback, one_recv.at[2])

        for h in range(heads):
            columns = slice(h * LANES, (h + 1) * LANES)
            rows = dot(pick(h, p.base, p.wide), wback[h]).astype(BF16)
            out_ref[:, columns] = out_ref[:, columns] + rows

    place_tokens(p, ids_ref, key_ref, wide_ref, place_ref)
    make_labels(p, ids_ref, wide_ref, place_ref, slab)
    pl.semaphore_wait(barrier, m_all - 1 + p.groups - 1)

    wide_at, lag, behind = 2, 4, 1

    downs = (g >= 2) & jnp.logical_not(lifts | pair_holder)

    def pass_on(c):
        @pl.when(downs)
        def _():
            wait_q(c)
            forward(c)

        @pl.when(lifts)
        def _():
            wait_kv(c)
            lift(c)

    send_labels()
    for load in loads:
        load.wait()

    @pl.loop(0, chunks)
    def _(c):
        pack(c)

        @pl.when(jnp.logical_not(lifts))
        def _():
            send_q(c)

        @pl.when(jnp.logical_not(downs))
        def _():
            send_kv(c)

        @pl.when(c == 1)
        def _():
            pack_wide()

        @pl.when(c == 1)
        def _():
            share_labels()

        @pl.when(c >= behind)
        def _():
            pass_on(c - behind)

        @pl.when((c == 3) & jnp.logical_not(pair_holder))
        def _():
            forward_wide()

    @pl.when(lifts)
    def _():
        @pl.loop(0, chunks)
        def _(c):
            send_q(c)

    @pl.when(downs)
    def _():
        @pl.loop(0, chunks)
        def _(c):
            send_kv(c)

    @pl.loop(chunks - behind, chunks)
    def _(c):
        pass_on(c)

    make_columns()

    @pl.when(pair_holder)
    def _():
        @pl.loop(0, chunks)
        def _(c):
            wait_q(c)
            forward(c)
            wait_kv(c)

            @pl.when(c == 0)
            def _():
                fetch_labels()

            @pl.when(c == 1)
            def _():
                forward_wide()

            visitors(c, True)
            own_part(c, True)

            @pl.when((c == wide_at) & is_wide)
            def _():
                wait_for(zwkv, up_recv.at[last])
                visitors_wide(True)
                own_wide(True)

            @pl.when((n_ret == 0) & (c >= lag))
            def _():
                unpack(c - lag)

    @pl.when(jnp.logical_not(pair_holder))
    def _():
        @pl.when(last_holder)
        def _():
            fetch_labels()

        @pl.loop(0, chunks)
        def _(c):
            @pl.when(lifts)
            def _():
                wait_q(c)
                forward(c)

            @pl.when(downs)
            def _():
                wait_kv(c)

            own_part(c, False)

            @pl.when(last_holder)
            def _():
                visitors(c, False)

            @pl.when((c == wide_at) & is_wide)
            def _():
                own_wide(False)

                @pl.when(last_holder)
                def _():
                    visitors_wide(False)

            @pl.when((n_ret == 0) & (c >= lag))
            def _():
                unpack(c - lag)

    @pl.when(n_ret == 0)
    def _():
        @pl.loop(chunks - lag, chunks - 1)
        def _(c):
            unpack(c)

    @pl.when(n_ret > 0)
    def _():
        @pl.loop(0, chunks)
        def _(c):
            combine(c)

            @pl.when((c == wide_at) & is_wide)
            def _():
                combine_wide()

            @pl.when(c > 0)
            def _():
                unpack(c - 1)

    unpack_wide()
    unpack(chunks - 1)

    @pl.loop(0, chunks)
    def _(c):
        wait_for(sq.at[c, pl.ds(0, m_all - 1)], plane_send.at[0, c])
        wait_for(skv.at[c, pl.ds(0, m_all - 1)], plane_send.at[1, c])
        wait_for(sa.at[c, :, pl.ds(0, m_all - 1)], plane_send.at[2, c])
        for i, holding in enumerate(p.holders):

            @pl.when(g > holding)
            def _():
                wait_for(rq.at[c], down_send.at[i, c])

        @pl.when(lifts)
        def _():
            wait_for(rkv.at[c], up_send.at[c])

        @pl.loop(0, n_sets)
        def _(s):
            wait_for(zq.at[s, c], ret_send.at[0, s, c])
            wait_for(pst.at[s, c, pl.ds(0, p.srows)], ret_send.at[1, s, c])

    for i, holding in enumerate(p.holders):

        @pl.when(g > holding)
        def _():
            wait_for(tab.at[g], tab_send.at[i])

    @pl.when(lifts)
    def _():
        wait_for(tab.at[g], tab_send.at[len(p.holders)])

    wait_for(slab.at[pl.ds(0, m_all - 1)], one_send.at[1])

    @pl.when(jnp.logical_not(is_wide))
    def _():
        wait_for(swb, one_send.at[0])

    @pl.when(is_wide)
    def _():
        wait_for(swb.at[pl.ds(0, heads - 1)], one_send.at[0])
        wait_for(swa.at[pl.ds(0, m_all - 1)], one_send.at[2])
        for i, holding in enumerate(p.holders):

            @pl.when(g > holding)
            def _():
                wait_for(rwb.at[0], down_send.at[i, chunks])

        @pl.when(lifts)
        def _():
            wait_for(zwkv, up_send.at[chunks])

        @pl.loop(0, n_sets)
        def _(s):
            wait_for(zwq.at[s], ret_send.at[0, s, chunks])
            wait_for(wst.at[s], ret_send.at[1, s, chunks])


VMEM_SPEC = pl.BlockSpec(memory_space=pltpu.VMEM)


def local(query_rows, key_rows, value_rows, cluster_ids):
    groups, members = lax.axis_size("grp"), lax.axis_size("ctx")
    heads, tokens = cluster_ids.shape
    p = Plan(groups, members, heads, tokens)
    c, rc, m, st, w = p.chunks, p.rc, p.members, p.stride, p.wide
    qs, ps, hold, tiles = p.qsets, p.psets, len(p.holders), c * rc + 1
    assert rc * p.rows // LANES <= 8 and p.wrows // LANES <= 8 and p.ranges * st <= LANES

    def half(*shape):
        return pltpu.VMEM((*shape, LANES), BF16)

    def full(*shape):
        return pltpu.VMEM((*shape, LANES), F32)

    ids = pltpu.VMEM((up(heads, 8), tokens), jnp.int32)
    dma = pltpu.SemaphoreType.DMA
    half_rows = pltpu.VMEM((tokens, heads * LANES), BF16)
    return pl.pallas_call(
        functools.partial(kernel, p),
        out_shape=jax.ShapeDtypeStruct((tokens, heads * LANES), BF16),
        in_specs=[VMEM_SPEC] + [pl.BlockSpec(memory_space=pl.ANY)] * 3,
        out_specs=VMEM_SPEC,
        scratch_shapes=[
            half_rows, half_rows, half_rows,
            ids, ids, ids, pltpu.VMEM((heads, tokens, LANES), jnp.int32),
            half(c, m, rc, st), half(c, m, 2, rc, st), half(heads, 3, w), half(m, SUB),
            half(c, rc, m, st), half(c, 2, rc, m, st), half(3, m, w), half(m, SUB),
            half(groups, p.table), full(groups, p.table),
            half(qs, c, rc, m, st), half(qs, m, w), half(c, 2, rc, m, st), half(2, m, w),
            full(qs, c, 8), full(qs, 8),
            half(ps, c, rc, m, st), half(ps, m, w), full(ps, c, 8), full(ps, 8),
            full(c, rc, p.rows), full(c, 8), full(p.wrows), full(8),
            half(c, m, rc, st), half(heads, w),
            dma((3,)), dma((3, c)), dma((3, c)), dma((3, c)), dma((3,)), dma((3,)), dma((3,)),
            dma((c + 1,)), dma((tiles,)), dma((hold, c + 1)), dma((qs, tiles)),
            dma((2, qs, c + 1)), dma((2, ps, tiles)), dma((hold + 1,)), dma((groups,)),
        ],
        compiler_params=pltpu.CompilerParams(
            collective_id=0, has_side_effects=True, vmem_limit_bytes=60 * 2**20
        ),
    )(cluster_ids, query_rows, key_rows, value_rows)


def solution(mesh):
    return jax.shard_map(
        local,
        mesh=mesh,
        in_specs=(
            P(("grp", "ctx"), None),
            P(("grp", "ctx"), None),
            P(("grp", "ctx"), None),
            P(None, ("grp", "ctx")),
        ),
        out_specs=P(("grp", "ctx"), None),
        check_vma=False,
    )
```

```python
import functools
import itertools
import math

import jax
import jax.numpy as jnp
from jax import lax
from jax.experimental import pallas as pl
from jax.experimental.pallas import tpu as pltpu
from jax.sharding import PartitionSpec as P

CL_SHIFT = 3
LANES = 128
SUB = 16
BLOCK = 256
NEG_FILL = -1e30
F32 = jnp.float32
BF16 = jnp.bfloat16
FACTOR = LANES**-0.5 * math.log2(math.e)
MESH = pl.DeviceIdType.MESH


def up(value, step):
    return (value + step - 1) // step * step


def shift_of(value):
    assert value & (value - 1) == 0
    return value.bit_length() - 1


class Plan:
    def __init__(self, groups, members, heads, tokens):
        self.groups, self.members, self.heads, self.tokens = groups, members, heads, tokens
        self.n = groups * members
        self.cap = tokens // self.n
        self.busy = 3 * tokens // self.n
        self.stride = up(self.cap, SUB)
        self.wide = up(self.busy, SUB)
        self.ranges = groups
        self.parts = 2
        self.rc = self.ranges // self.parts
        self.chunks = heads * self.parts
        self.rows = members * self.stride
        self.mrows = self.rc * self.stride
        self.crows = members * self.mrows
        self.srows = self.rc * self.rows // LANES
        self.wrows = members * self.wide
        self.base = self.n * self.stride
        self.spread = members // heads
        self.table = up((heads + 1) * members, SUB)
        self.holders = [c for c in range(1, groups - 2, 2)] + [groups - 2]
        self.qsets = groups - 2
        self.psets = groups // 2


def iota(shape, dim):
    return lax.broadcasted_iota(jnp.int32, shape, dim)


def dot(a, b):
    return jnp.dot(a, b, preferred_element_type=F32)


def dot_t(a, b):
    return lax.dot_general(a, b, (((1,), (1,)), ((), ())), preferred_element_type=F32)


def onehot(cond):
    return jnp.where(cond, 1.0, 0.0).astype(BF16)


def place_tokens(p, ids_ref, key_ref, wide_ref, place_ref):
    n, t = p.n, p.tokens
    blk = math.gcd(BLOCK, t)
    earlier = onehot(iota((blk, blk), 0) < iota((blk, blk), 1))
    owners, members = [], []
    for h in range(p.heads):
        owner = lax.shift_right_logical(ids_ref[h : h + 1, :], CL_SHIFT)
        owners.append(owner)
        members.append(jnp.where(iota((n, t), 0) == owner, 1.0, 0.0))
    member = jnp.concatenate(members, axis=0)
    carry = jnp.zeros((p.heads * n, 1), F32)
    slots = []
    for b in range(0, t, blk):
        piece = member[:, b : b + blk]
        slots.append(piece * (dot(piece.astype(BF16), earlier) + carry))
        carry += jnp.sum(piece, axis=1, keepdims=True)
    slot_all = jnp.concatenate(slots, axis=1)
    full = jnp.where(carry > p.cap, 1.0, 0.0)
    for h in range(p.heads):
        rows = slice(h * n, (h + 1) * n)
        owner = owners[h]
        slot = jnp.sum(slot_all[rows], axis=0, keepdims=True).astype(jnp.int32)
        is_busy = jnp.sum(members[h] * full[rows], axis=0, keepdims=True) > 0.5
        who = lax.shift_right_logical(owner, shift_of(p.ranges))
        which = owner & (p.ranges - 1)
        part = lax.shift_right_logical(which, shift_of(p.rc))
        row = part * p.crows + who * p.mrows + (which & (p.rc - 1)) * p.stride + slot
        key_ref[h : h + 1, :] = jnp.where(is_busy, p.base + slot, row)
        wide_ref[h : h + 1, :] = jnp.where(is_busy, slot, -1)
        place_ref[h : h + 1, :] = jnp.where(is_busy, -1, which * p.stride + slot)


def make_labels(p, ids_ref, wide_ref, place_ref, slab_ref):
    m, t = p.members, p.tokens
    row = iota((m * SUB, m), 0) - iota((m * SUB, m), 1) * SUB
    spread = jnp.zeros((m * SUB, LANES), F32)
    for h in range(p.heads):
        ids = ids_ref[h : h + 1, :]
        who = lax.shift_right_logical(ids, CL_SHIFT + shift_of(p.ranges))
        label = ((ids & (2**CL_SHIFT - 1)) + 1).astype(F32)
        mine = jnp.where(iota((m, t), 0) == who, label, 0.0).astype(BF16)
        spot = onehot(iota((LANES, t), 0) == place_ref[h : h + 1, :])
        spread += dot(onehot(row == h), dot_t(mine, spot).astype(BF16))
        spot = onehot(iota((LANES, t), 0) == wide_ref[h : h + 1, :])
        line = dot_t(jnp.broadcast_to(label, (m, t)).astype(BF16), spot)
        line = jnp.where(iota((m, LANES), 0) == h * p.spread, line, 0.0)
        spread += dot(onehot(row == p.heads), line.astype(BF16))
    slab_ref[...] = spread.astype(BF16).reshape(m, SUB, LANES)


def read_labels(p, rlab_ref):
    m = p.members
    total = m * SUB
    want = iota((p.table, total), 0)
    src, h = want & (m - 1), lax.shift_right_logical(want, shift_of(m))
    pick = onehot((iota((p.table, total), 1) == src * SUB + h) & (h <= p.heads))
    return dot(pick, rlab_ref[...].reshape(total, LANES))


def row_labels(table, width, offset):
    m = table.shape[0]
    total = m * width
    src = iota((m, width, m), 0).reshape(total, m)
    spread = dot(onehot(src == iota((total, m), 1)), table.astype(BF16))
    lane = iota((m, width, LANES), 1).reshape(total, LANES) + offset
    return jnp.sum(
        jnp.where(iota((total, LANES), 1) == lane, spread, 0.0), axis=1, keepdims=True
    )


def lane_labels(table, width, offset):
    m = table.shape[0]
    total = m * width
    lane = iota((1, total), 1)
    src = jnp.floor((lane.astype(F32) + 0.5) * (1.0 / width)).astype(jnp.int32)
    spot = onehot(iota((LANES, total), 0) == lane - src * width + offset)
    spread = dot(table.astype(BF16), spot)
    return jnp.sum(jnp.where(iota((m, total), 0) == src, spread, 0.0), axis=0, keepdims=True)


def attend(queries, parts):
    masked = [jnp.where(ok, dot_t(queries, k), NEG_FILL) for k, _, ok in parts]
    top = functools.reduce(jnp.maximum, [jnp.max(s, axis=1, keepdims=True) for s in masked])
    weights = [jnp.exp2((s - top) * FACTOR) for s in masked]
    total = sum(jnp.sum(w, axis=1, keepdims=True) for w in weights)
    acc = sum(dot(w.astype(BF16), v) for w, (_, v, _) in zip(weights, parts))
    return acc * (1.0 / total), top * FACTOR + jnp.log2(total)


def to_rows(column):
    count = column.shape[0] // LANES
    wide = jnp.broadcast_to(column, (column.shape[0], LANES)).reshape(count, LANES, LANES)
    eye = iota((count, LANES, LANES), 1) == iota((count, LANES, LANES), 2)
    return jnp.sum(jnp.where(eye, wide, 0.0), axis=1)


def to_columns(row):
    return jnp.transpose(jnp.broadcast_to(row, (LANES, LANES)))


def kernel(
    p, ids_ref, q_hbm, k_hbm, v_hbm, out_ref, q_ref, k_ref, v_ref,
    key_ref, wide_ref, place_ref, kcol_ref,
    sq, skv, swb, slab, rq, rkv, rwb, rlab, tab, tabf,
    zq, zwq, zkv, zwkv, pst, wst, pin, wpin, pinst, wpinst,
    loc, locst, wloc, wlocst, back, wback,
    load_sem, plane_send, plane_recv, plane_own, one_send, one_recv, one_own,
    up_send, up_recv, down_send, down_recv, ret_send, ret_recv, tab_send, tab_recv,
):
    m_all, heads, chunks = p.members, p.heads, p.chunks
    g, m = lax.axis_index("grp"), lax.axis_index("ctx")
    pair_holder = (g < p.groups - 2) & (lax.rem(g, 2) == 1)
    last_holder = g == p.groups - 2
    holder = pair_holder | last_holder
    lifts = (g < p.groups - 2) & (lax.rem(g, 2) == 0)
    n_sets = jnp.where(holder, p.groups - 1 - g, 0)
    n_ret = lax.div(jnp.minimum(g, p.groups - 2), 2) + jnp.where(g == p.groups - 1, 1, 0)
    is_wide = lax.rem(m, p.spread) == 0
    sa, swa = pin.at[0], wpin.at[0]
    head_of = lax.div(m, p.spread)
    last = chunks * p.rc

    def member(step):
        return lax.rem(m + step, m_all)

    def remote(src, dst, send, recv, plane, who):
        return pltpu.make_async_remote_copy(
            src_ref=src, dst_ref=dst, send_sem=send, recv_sem=recv,
            device_id=(plane, who), device_id_type=MESH,
        )

    def wait_for(ref, sem):
        pltpu.make_async_copy(ref, ref, sem).wait()

    loads = [
        pltpu.make_async_copy(src, dst, load_sem.at[i])
        for i, (src, dst) in enumerate([(q_hbm, q_ref), (k_hbm, k_ref), (v_hbm, v_ref)])
    ]
    for load in loads:
        load.start()

    barrier = pltpu.get_barrier_semaphore()

    @pl.loop(1, m_all)
    def _(step):
        pl.semaphore_signal(barrier, inc=1, device_id=(g, member(step)), device_id_type=MESH)

    @pl.loop(1, p.groups)
    def _(step):
        pl.semaphore_signal(
            barrier, inc=1, device_id=(lax.rem(g + step, p.groups), m), device_id_type=MESH
        )

    def spread_out(kind, c, src_of, dst, own_src, own_dst):
        @pl.loop(1, m_all)
        def _(step):
            other = member(step)
            remote(
                src_of(other), dst, plane_send.at[kind, c], plane_recv.at[kind, c], g, other
            ).start()

        pltpu.make_async_copy(own_src, own_dst, plane_own.at[kind, c]).start()

    def send_q(c):
        spread_out(0, c, lambda o: sq.at[c, o], rq.at[c, :, m], sq.at[c, m], rq.at[c, :, m])

    def send_kv(c):
        spread_out(
            1, c, lambda o: skv.at[c, o], rkv.at[c, :, :, m], skv.at[c, m], rkv.at[c, :, :, m]
        )

    def send_answers(c, j):
        mine = back.at[c, m, j]
        spread_out(2, c, lambda o: sa.at[c, j, o], mine, sa.at[c, j, m], mine)

    def wait_q(c):
        wait_for(rq.at[c, :, pl.ds(0, m_all - 1)], plane_recv.at[0, c])
        wait_for(rq.at[c, :, m], plane_own.at[0, c])

    def wait_kv(c):
        wait_for(rkv.at[c, :, :, pl.ds(0, m_all - 1)], plane_recv.at[1, c])
        wait_for(rkv.at[c, :, :, m], plane_own.at[1, c])

    def wait_answers(c):
        wait_for(back.at[c, pl.ds(0, m_all - 1)], plane_recv.at[2, c])
        wait_for(back.at[c, m], plane_own.at[2, c])

    def pack(c):
        h, part = lax.div(c, p.parts), lax.rem(c, p.parts)
        columns = pl.ds(pl.multiple_of(h * LANES, LANES), LANES)
        data = jnp.concatenate([q_ref[:, columns], k_ref[:, columns], v_ref[:, columns]], axis=1)
        select = onehot(
            iota((p.crows, p.tokens), 0) + part * p.crows == key_ref[pl.ds(h, 1), :]
        )
        moved = dot(select, data).astype(BF16)
        shape = (m_all, p.rc, p.stride, LANES)
        sq[c] = moved[:, :LANES].reshape(shape)
        skv[c, :, 0] = moved[:, LANES : 2 * LANES].reshape(shape)
        skv[c, :, 1] = moved[:, 2 * LANES :].reshape(shape)

    def pack_wide():
        for h in range(heads):
            columns = slice(h * LANES, (h + 1) * LANES)
            data = jnp.concatenate(
                [q_ref[:, columns], k_ref[:, columns], v_ref[:, columns]], axis=1
            )
            select = onehot(iota((p.wide, p.tokens), 0) == wide_ref[h : h + 1, :])
            moved = dot(select, data).astype(BF16)
            for i in range(3):
                swb[h, i] = moved[:, i * LANES : (i + 1) * LANES]
            target = h * p.spread

            @pl.when(m == target)
            def _():
                pltpu.make_async_copy(swb.at[h], rwb.at[:, m], one_own.at[0]).start()

            @pl.when(m != target)
            def _():
                remote(
                    swb.at[h], rwb.at[:, m], one_send.at[0], one_recv.at[0], g, target
                ).start()

    def wait_wide():
        wait_for(rwb.at[:, pl.ds(0, m_all - 1)], one_recv.at[0])
        wait_for(rwb.at[:, m], one_own.at[0])

    def send_labels():
        @pl.loop(1, m_all)
        def _(step):
            other = member(step)
            remote(slab.at[other], rlab.at[m], one_send.at[1], one_recv.at[1], g, other).start()

        pltpu.make_async_copy(slab.at[m], rlab.at[m], one_own.at[1]).start()

    def share_labels():
        wait_for(rlab.at[pl.ds(0, m_all - 1)], one_recv.at[1])
        wait_for(rlab.at[m], one_own.at[1])
        mine = read_labels(p, rlab)
        tabf[g] = mine
        tab[g] = mine.astype(BF16)
        for c, holding in enumerate(p.holders):

            @pl.when(g > holding)
            def _():
                remote(tab.at[g], tab.at[g], tab_send.at[c], tab_recv.at[g], holding, m).start()

        @pl.when(lifts)
        def _():
            remote(
                tab.at[g], tab.at[g], tab_send.at[len(p.holders)], tab_recv.at[g], g + 1, m
            ).start()

    def fetch_labels():
        def fetch(s):
            wait_for(tab.at[s], tab_recv.at[s])
            tabf[s] = tab[s].astype(F32)

        @pl.when(pair_holder)
        def _():
            fetch(g - 1)

        @pl.loop(0, n_sets)
        def _(i):
            fetch(g + 1 + i)

    def forward(c):
        for j, (i, holding) in itertools.product(range(p.rc), enumerate(p.holders)):

            @pl.when(g > holding)
            def _():
                s = g - holding - 1
                remote(
                    rq.at[c, j], zq.at[s, c, j], down_send.at[i, c],
                    down_recv.at[s, c * p.rc + j], holding, m,
                ).start()

    def lift(c):
        @pl.when(lifts)
        def _():
            for j in range(p.rc):
                remote(
                    rkv.at[c, :, j], zkv.at[c, :, j], up_send.at[c],
                    up_recv.at[c * p.rc + j], g + 1, m,
                ).start()

    def forward_wide():
        @pl.when(is_wide)
        def _():
            wait_wide()
            for i, holding in enumerate(p.holders):

                @pl.when(g > holding)
                def _():
                    s = g - holding - 1
                    remote(
                        rwb.at[0], zwq.at[s], down_send.at[i, chunks],
                        down_recv.at[s, last], holding, m,
                    ).start()

            @pl.when(lifts)
            def _():
                remote(
                    rwb.at[pl.ds(1, 2)], zwkv, up_send.at[chunks], up_recv.at[last], g + 1, m
                ).start()

    def tables(s, h):
        return tabf[s, pl.ds(pl.multiple_of(h * m_all, m_all), m_all), :]

    def flat(value):
        return value.reshape(-1, LANES)

    def causal(size, keys, first):
        return iota((size, keys), 1) <= iota((size, keys), 0) + first

    def give_back(src, dst_of, kind, s, sent, slot):
        where = jnp.where(last_holder, p.psets - 1, lax.div(g - 1, 2))
        remote(
            src, dst_of(where), ret_send.at[kind, s, sent], ret_recv.at[kind, where, slot],
            g + 1 + s, m,
        ).start()

    def tile_of(c):
        return lax.div(c, p.parts), lax.rem(c, p.parts) * p.rc

    def own_part(c, with_before):
        h, r = tile_of(c)
        for j in range(p.rc):
            offset = (r + j) * p.stride
            table = tables(g, h)
            lq, lk = row_labels(table, p.stride, offset), lane_labels(table, p.stride, offset)
            ok = (lq == lk) & causal(p.rows, p.rows, 0)
            parts = [(flat(rkv[c, 0, j]), flat(rkv[c, 1, j]), ok)]
            if with_before:
                before = lane_labels(tables(g - 1, h), p.stride, offset)
                parts.append((flat(zkv[c, 0, j]), flat(zkv[c, 1, j]), lq == before))
            out, lse = attend(flat(rq[c, j]), parts)

            @pl.when(n_ret == 0)
            def _():
                sa[c, j] = out.astype(BF16).reshape(m_all, p.stride, LANES)
                send_answers(c, j)

            @pl.when(n_ret > 0)
            def _():
                loc[c, j] = out
                count = p.rows // LANES
                locst[c, j * count : (j + 1) * count, :] = to_rows(lse)

    def visitors(c, with_before):
        h, r = tile_of(c)
        count = p.rows // LANES
        for j in range(p.rc):
            offset = (r + j) * p.stride
            slot = c * p.rc + j
            if with_before:
                wait_for(zkv.at[c, :, j], up_recv.at[slot])

            @pl.loop(0, n_sets)
            def _(s):
                wait_for(zq.at[s, c, j], down_recv.at[s, slot])
                lq = row_labels(tables(g + 1 + s, h), p.stride, offset)
                lk = lane_labels(tables(g, h), p.stride, offset)
                parts = [(flat(rkv[c, 0, j]), flat(rkv[c, 1, j]), lq == lk)]
                if with_before:
                    before = lane_labels(tables(g - 1, h), p.stride, offset)
                    parts.append((flat(zkv[c, 0, j]), flat(zkv[c, 1, j]), lq == before))
                out, lse = attend(flat(zq[s, c, j]), parts)
                zq[s, c, j] = out.astype(BF16).reshape(m_all, p.stride, LANES)
                pst[s, c, j * count : (j + 1) * count, :] = to_rows(lse)
                give_back(zq.at[s, c, j], lambda w: pin.at[w, c, j], 0, s, c, slot)
                if j == p.rc - 1:
                    stats = pl.ds(0, p.srows)
                    give_back(
                        pst.at[s, c, stats], lambda w: pinst.at[w, c, stats], 1, s, c, c
                    )

    def wide_blocks():
        size = math.gcd(BLOCK, p.wrows)
        return size, range(0, p.wrows, size)

    def own_wide(with_before):
        size, starts = wide_blocks()
        table = tables(g, heads)
        lq_all, lk_all = row_labels(table, p.wide, 0), lane_labels(table, p.wide, 0)
        queries = flat(rwb[0])
        keys, values = flat(rwb[1]), flat(rwb[2])
        outs, lses = [], []
        for first in starts:
            lq = lq_all[first : first + size]
            end = first + size
            ok = (lq == lk_all[:, :end]) & causal(size, end, first)
            parts = [(keys[:end], values[:end], ok)]
            if with_before:
                before = lane_labels(tables(g - 1, heads), p.wide, 0)
                parts.append((flat(zwkv[0]), flat(zwkv[1]), lq == before))
            out, lse = attend(queries[first:end], parts)
            outs.append(out)
            lses.append(to_rows(lse))
        out = jnp.concatenate(outs, axis=0)

        @pl.when(n_ret == 0)
        def _():
            swa[...] = out.astype(BF16).reshape(m_all, p.wide, LANES)
            send_wide()

        @pl.when(n_ret > 0)
        def _():
            wloc[...] = out
            wlocst[0 : p.wrows // LANES, :] = jnp.concatenate(lses, axis=0)

    def visitors_wide(with_before):
        size, starts = wide_blocks()

        @pl.loop(0, n_sets)
        def _(s):
            wait_for(zwq.at[s], down_recv.at[s, last])
            lq_all = row_labels(tables(g + 1 + s, heads), p.wide, 0)
            lk = lane_labels(tables(g, heads), p.wide, 0)
            queries = flat(zwq[s])
            outs, lses = [], []
            for first in starts:
                lq = lq_all[first : first + size]
                parts = [(flat(rwb[1]), flat(rwb[2]), lq == lk)]
                if with_before:
                    before = lane_labels(tables(g - 1, heads), p.wide, 0)
                    parts.append((flat(zwkv[0]), flat(zwkv[1]), lq == before))
                out, lse = attend(queries[first : first + size], parts)
                outs.append(out.astype(BF16))
                lses.append(to_rows(lse))
            zwq[s] = jnp.concatenate(outs, axis=0).reshape(m_all, p.wide, LANES)
            wst[s, 0 : p.wrows // LANES, :] = jnp.concatenate(lses, axis=0)
            give_back(zwq.at[s], lambda w: wpin.at[w], 0, s, chunks, last)
            give_back(wst.at[s], lambda w: wpinst.at[w], 1, s, chunks, chunks)

    def send_wide():
        @pl.loop(1, m_all)
        def _(step):
            other = member(step)
            remote(
                swa.at[other], wback.at[head_of], one_send.at[2], one_recv.at[2], g, other
            ).start()

        pltpu.make_async_copy(swa.at[m], wback.at[head_of], one_own.at[2]).start()

    def merge(outs, lses):
        top = functools.reduce(jnp.maximum, lses)
        weights = [jnp.exp2(x - top) for x in lses]
        share = 1.0 / sum(weights)
        weights = [w * share for w in weights]
        blocks = []
        for i in range(weights[0].shape[0]):
            rows = slice(i * LANES, (i + 1) * LANES)
            blocks.append(sum(to_columns(w[i : i + 1]) * o[rows] for w, o in zip(weights, outs)))
        return jnp.concatenate(blocks, axis=0).astype(BF16)

    def combine(c):
        for k in range(1, p.psets + 1):

            @pl.when(n_ret == k)
            def _():
                for i in range(k):
                    wait_for(pinst.at[i, c, pl.ds(0, p.srows)], ret_recv.at[1, i, c])
                count = p.rows // LANES
                for j in range(p.rc):
                    for i in range(k):
                        wait_for(pin.at[i, c, j], ret_recv.at[0, i, c * p.rc + j])
                    rows = slice(j * count, (j + 1) * count)
                    outs = [loc[c, j]] + [flat(pin[i, c, j]) for i in range(k)]
                    lses = [locst[c, rows, :]] + [pinst[i, c, rows, :] for i in range(k)]
                    sa[c, j] = merge(outs, lses).reshape(m_all, p.stride, LANES)
                    send_answers(c, j)

    def combine_wide():
        for k in range(1, p.psets + 1):

            @pl.when(n_ret == k)
            def _():
                for i in range(k):
                    wait_for(wpin.at[i], ret_recv.at[0, i, last])
                    wait_for(wpinst.at[i], ret_recv.at[1, i, chunks])
                count = p.wrows // LANES
                outs = [wloc[...]] + [flat(wpin[i]) for i in range(k)]
                lses = [wlocst[:count, :]] + [wpinst[i, :count, :] for i in range(k)]
                swa[...] = merge(outs, lses).reshape(m_all, p.wide, LANES)

        send_wide()

    def make_columns():
        for h in range(heads):
            line = jnp.broadcast_to(key_ref[h : h + 1, :].astype(F32), (LANES, p.tokens))
            kcol_ref[h] = jnp.transpose(line).astype(jnp.int32)

    def pick(h, first, count):
        pieces = []
        for at in range(0, count, LANES):
            width = min(LANES, count - at)
            lane = iota((p.tokens, width), 1) + (first + at)
            pieces.append(onehot(lane == kcol_ref[h, :, :width]))
        return jnp.concatenate(pieces, axis=1)

    def unpack(c):
        wait_answers(c)
        h, part = lax.div(c, p.parts), lax.rem(c, p.parts)
        columns = pl.ds(pl.multiple_of(h * LANES, LANES), LANES)
        rows = dot(pick(h, part * p.crows, p.crows), flat(back[c])).astype(BF16)

        @pl.when(part == 0)
        def _():
            out_ref[:, columns] = rows

        @pl.when(part > 0)
        def _():
            out_ref[:, columns] = out_ref[:, columns] + rows

    def unpack_wide():
        @pl.when(is_wide)
        def _():
            wait_for(wback.at[pl.ds(0, heads - 1)], one_recv.at[2])
            wait_for(wback.at[head_of], one_own.at[2])

        @pl.when(jnp.logical_not(is_wide))
        def _():
            wait_for(wback, one_recv.at[2])

        for h in range(heads):
            columns = slice(h * LANES, (h + 1) * LANES)
            rows = dot(pick(h, p.base, p.wide), wback[h]).astype(BF16)
            out_ref[:, columns] = out_ref[:, columns] + rows

    place_tokens(p, ids_ref, key_ref, wide_ref, place_ref)
    make_labels(p, ids_ref, wide_ref, place_ref, slab)
    pl.semaphore_wait(barrier, m_all - 1 + p.groups - 1)

    wide_at, lag, behind, late = 2, 4, 1, 2

    downs = (g >= 2) & jnp.logical_not(lifts | pair_holder)

    def pass_on(c):
        @pl.when(downs)
        def _():
            wait_q(c)
            forward(c)

        @pl.when(lifts)
        def _():
            wait_kv(c)
            lift(c)

    send_labels()
    for load in loads:
        load.wait()

    @pl.loop(0, chunks)
    def _(c):
        pack(c)

        @pl.when(jnp.logical_not(lifts))
        def _():
            send_q(c)

        @pl.when(jnp.logical_not(downs))
        def _():
            send_kv(c)

        @pl.when(c == 1)
        def _():
            pack_wide()

        @pl.when(c == 1)
        def _():
            share_labels()

        @pl.when(c >= behind)
        def _():
            pass_on(c - behind)

        @pl.when((c == 3) & jnp.logical_not(pair_holder))
        def _():
            forward_wide()

    @pl.when(lifts)
    def _():
        @pl.loop(0, chunks)
        def _(c):
            send_q(c)

    @pl.when(downs)
    def _():
        @pl.loop(0, chunks)
        def _(c):
            send_kv(c)

    @pl.loop(chunks - behind, chunks)
    def _(c):
        pass_on(c)

    make_columns()

    @pl.when(pair_holder)
    def _():
        @pl.loop(0, chunks)
        def _(c):
            wait_q(c)
            forward(c)
            wait_kv(c)

            @pl.when(c == 0)
            def _():
                fetch_labels()

            @pl.when(c == 1)
            def _():
                forward_wide()

            visitors(c, True)
            own_part(c, True)

            @pl.when((c == wide_at) & is_wide)
            def _():
                wait_for(zwkv, up_recv.at[last])
                visitors_wide(True)
                own_wide(True)

            @pl.when((n_ret == 0) & (c >= lag))
            def _():
                unpack(c - lag)

    @pl.when(jnp.logical_not(pair_holder))
    def _():
        @pl.when(last_holder)
        def _():
            fetch_labels()

        @pl.loop(0, chunks)
        def _(c):
            @pl.when(lifts)
            def _():
                wait_q(c)
                forward(c)

            @pl.when(downs)
            def _():
                wait_kv(c)

            own_part(c, False)

            @pl.when(last_holder)
            def _():
                visitors(c, False)

            @pl.when((c == wide_at) & is_wide)
            def _():
                own_wide(False)

                @pl.when(last_holder)
                def _():
                    visitors_wide(False)

            @pl.when((n_ret == 0) & (c >= lag))
            def _():
                unpack(c - lag)

    @pl.when(n_ret == 0)
    def _():
        @pl.loop(chunks - lag, chunks - 1)
        def _(c):
            unpack(c)

    @pl.when(n_ret > 0)
    def _():
        @pl.loop(0, chunks)
        def _(c):
            combine(c)

            @pl.when((c == wide_at) & is_wide)
            def _():
                combine_wide()

            @pl.when(c >= late)
            def _():
                unpack(c - late)

        @pl.loop(chunks - late, chunks - 1)
        def _(c):
            unpack(c)

    unpack_wide()
    unpack(chunks - 1)

    @pl.loop(0, chunks)
    def _(c):
        wait_for(sq.at[c, pl.ds(0, m_all - 1)], plane_send.at[0, c])
        wait_for(skv.at[c, pl.ds(0, m_all - 1)], plane_send.at[1, c])
        wait_for(sa.at[c, :, pl.ds(0, m_all - 1)], plane_send.at[2, c])
        for i, holding in enumerate(p.holders):

            @pl.when(g > holding)
            def _():
                wait_for(rq.at[c], down_send.at[i, c])

        @pl.when(lifts)
        def _():
            wait_for(rkv.at[c], up_send.at[c])

        @pl.loop(0, n_sets)
        def _(s):
            wait_for(zq.at[s, c], ret_send.at[0, s, c])
            wait_for(pst.at[s, c, pl.ds(0, p.srows)], ret_send.at[1, s, c])

    for i, holding in enumerate(p.holders):

        @pl.when(g > holding)
        def _():
            wait_for(tab.at[g], tab_send.at[i])

    @pl.when(lifts)
    def _():
        wait_for(tab.at[g], tab_send.at[len(p.holders)])

    wait_for(slab.at[pl.ds(0, m_all - 1)], one_send.at[1])

    @pl.when(jnp.logical_not(is_wide))
    def _():
        wait_for(swb, one_send.at[0])

    @pl.when(is_wide)
    def _():
        wait_for(swb.at[pl.ds(0, heads - 1)], one_send.at[0])
        wait_for(swa.at[pl.ds(0, m_all - 1)], one_send.at[2])
        for i, holding in enumerate(p.holders):

            @pl.when(g > holding)
            def _():
                wait_for(rwb.at[0], down_send.at[i, chunks])

        @pl.when(lifts)
        def _():
            wait_for(zwkv, up_send.at[chunks])

        @pl.loop(0, n_sets)
        def _(s):
            wait_for(zwq.at[s], ret_send.at[0, s, chunks])
            wait_for(wst.at[s], ret_send.at[1, s, chunks])


VMEM_SPEC = pl.BlockSpec(memory_space=pltpu.VMEM)


def local(query_rows, key_rows, value_rows, cluster_ids):
    groups, members = lax.axis_size("grp"), lax.axis_size("ctx")
    heads, tokens = cluster_ids.shape
    p = Plan(groups, members, heads, tokens)
    c, rc, m, st, w = p.chunks, p.rc, p.members, p.stride, p.wide
    qs, ps, hold, tiles = p.qsets, p.psets, len(p.holders), c * rc + 1
    assert rc * p.rows // LANES <= 8 and p.wrows // LANES <= 8 and p.ranges * st <= LANES

    def half(*shape):
        return pltpu.VMEM((*shape, LANES), BF16)

    def full(*shape):
        return pltpu.VMEM((*shape, LANES), F32)

    ids = pltpu.VMEM((up(heads, 8), tokens), jnp.int32)
    dma = pltpu.SemaphoreType.DMA
    half_rows = pltpu.VMEM((tokens, heads * LANES), BF16)
    return pl.pallas_call(
        functools.partial(kernel, p),
        out_shape=jax.ShapeDtypeStruct((tokens, heads * LANES), BF16),
        in_specs=[VMEM_SPEC] + [pl.BlockSpec(memory_space=pl.ANY)] * 3,
        out_specs=VMEM_SPEC,
        scratch_shapes=[
            half_rows, half_rows, half_rows,
            ids, ids, ids, pltpu.VMEM((heads, tokens, LANES), jnp.int32),
            half(c, m, rc, st), half(c, m, 2, rc, st), half(heads, 3, w), half(m, SUB),
            half(c, rc, m, st), half(c, 2, rc, m, st), half(3, m, w), half(m, SUB),
            half(groups, p.table), full(groups, p.table),
            half(qs, c, rc, m, st), half(qs, m, w), half(c, 2, rc, m, st), half(2, m, w),
            full(qs, c, 8), full(qs, 8),
            half(ps, c, rc, m, st), half(ps, m, w), full(ps, c, 8), full(ps, 8),
            full(c, rc, p.rows), full(c, 8), full(p.wrows), full(8),
            half(c, m, rc, st), half(heads, w),
            dma((3,)), dma((3, c)), dma((3, c)), dma((3, c)), dma((3,)), dma((3,)), dma((3,)),
            dma((c + 1,)), dma((tiles,)), dma((hold, c + 1)), dma((qs, tiles)),
            dma((2, qs, c + 1)), dma((2, ps, tiles)), dma((hold + 1,)), dma((groups,)),
        ],
        compiler_params=pltpu.CompilerParams(
            collective_id=0, has_side_effects=True, vmem_limit_bytes=60 * 2**20
        ),
    )(cluster_ids, query_rows, key_rows, value_rows)


def solution(mesh):
    return jax.shard_map(
        local,
        mesh=mesh,
        in_specs=(
            P(("grp", "ctx"), None),
            P(("grp", "ctx"), None),
            P(("grp", "ctx"), None),
            P(None, ("grp", "ctx")),
        ),
        out_specs=P(("grp", "ctx"), None),
        check_vma=False,
    )
```
